256 devices in a mesh: gx: 16 (over z_hi, x), gy: 16 (over y, z_lo, core).
Axes of the slice: x: 4, y: 4, z: 8 (z_hi: 4, z_lo: 2; z = z_hi * 2 + z_lo), core: 2. Of those that a mesh axis runs over, the one named last changes fastest.
Arguments:
- profiles: float32 [2, 262144, 128], P(None, ('gx', 'gy')), may hold values from 0.5 to 2
- radial: float32 [2, 128, 128], replicated, may hold values from -1 to 2
- rate_const: float32 [262144], P(('gx', 'gy')), may hold values from 0.02 to 0.2
- transfer_coef: float32 [262144], P(('gx', 'gy')), may hold values from 0.1 to 0.5
- live_count: int32 [256], P(('gx', 'gy')), may hold values from 256 to 1024, as said below
- send_lists: int32 [2048, 128], P(('gx', 'gy')), may hold values from 0 to 1023, as said below
- cell_index: int32 [262144], P(('gx', 'gy')), may hold values from 0 to 131071
- contact_cols: int32 [2048, 4], P(('gx', 'gy')), may hold values from 0 to 15, as said below
- contact_blocks: float32 [2048, 4, 128, 128], P(('gx', 'gy')), may hold values from 0 to 0.006
- populations: float32 [7, 512, 512, 128], P(None, 'gx', 'gy'), may hold values from -1.8 to 1.8
Outputs:
- profiles_out: float32 [2, 262144, 128], P(None, ('gx', 'gy'))
- populations_out: float32 [7, 512, 512, 128], P(None, 'gx', 'gy')
The draws below stay inside these ranges and needn't reach their ends.
Inputs may be any that keep to these rules, and one draw needn't show every extreme that they name: `live_count`: each tile's count is a multiple of 128, at least a quarter of its slots, and some tile is full. `send_lists`: every entry names a live slot of the sending tile. `contact_cols`: blocks 0 to 7 are the tile's own, block 8 + n is ghost block n; every ghost block is named by some row block.
All inputs are finite; a program needn't handle non-finite values.
Results may differ from the reference program's by a relative error of at most 0.0001.
Values sent between devices are 32-bit elements; how exact they have to be, the bound alone decides.
No kernel may reach another device: no remote copies, remote signals or barrier semaphores. Data moves between devices by JAX's collectives and lax.ppermute only.
A program may use at most 128 MiB of HBM per device.

```python
import math
import jax
import jax.numpy as jnp
import numpy as np
from jax import lax

NR = 128
BLK = 128
SHELL = 16
KB = 4
STEPS = 3
PBLK = 8
CX = 32
CY = 32
NZ = 128
PELLETS = 262144
NX = 512
NY = 512
N_GX = 16
N_GY = 16


def live_helper(key):
    devices = N_GX * N_GY
    blocks = jax.random.randint(jax.random.fold_in(key, 11), (devices,), max(1, PBLK // 4), PBLK + 1)
    chosen_device = jax.random.randint(jax.random.fold_in(key, 12), (), 0, devices)
    counts = jnp.where(jnp.arange(devices) == chosen_device, PBLK, blocks) * BLK
    return counts.astype(jnp.int32)


def draw_live_count(key, part):
    return live_helper(key)


def draw_send_lists(key, part):
    devices = N_GX * N_GY
    counts = live_helper(key)
    entries = jax.random.randint(jax.random.fold_in(key, 13), (devices, 8, BLK), 0, counts[:, None, None])
    return entries.reshape(devices * 8, BLK).astype(jnp.int32)


def draw_contact_cols(key, part):
    devices = N_GX * N_GY
    rows = jnp.arange(PBLK, dtype=jnp.int32)
    own_block = jnp.broadcast_to(rows[None, :], (devices, PBLK))
    first_ghost = jnp.broadcast_to((PBLK + 2 * rows % 8)[None, :], (devices, PBLK))
    second_ghost = jnp.broadcast_to((PBLK + (2 * rows + 1) % 8)[None, :], (devices, PBLK))
    extra_block = jax.random.randint(jax.random.fold_in(key, 21), (devices, PBLK), 0, PBLK + 8)
    stacked = jnp.stack([own_block, first_ghost, second_ghost, extra_block], axis=2)
    return stacked.reshape(devices * PBLK, 4).astype(jnp.int32)


def draw_radial(key, part):
    diag_key = jax.random.fold_in(key, 31)
    off_key = jax.random.fold_in(key, 32)
    diagonal_part = jax.random.uniform(diag_key, (2, NR), minval=0.55, maxval=0.95)
    spread = jnp.clip(jax.random.normal(off_key, (2, NR, NR)), -4.0, 4.0) * (0.3 / math.sqrt(NR))
    return (spread + jnp.eye(NR, dtype=jnp.float32)[None] * diagonal_part[:, :, None]).astype(jnp.float32)


def set_ends(values, stream_key, least, largest):
    spot = [jax.random.randint(jax.random.fold_in(stream_key, axis), (), 0, length) for axis, length in enumerate(values.shape)]
    widest = values.shape.index(max(values.shape))
    neighbour = spot[:widest] + [(spot[widest] + 1) % values.shape[widest]] + spot[widest + 1:]
    return values.at[tuple(spot)].set(least).at[tuple(neighbour)].set(largest)


def shard_levels(rng, shape, pieces, least, largest):
    def one(position, blocks):
        steps = jax.random.uniform(jax.random.fold_in(jax.random.fold_in(rng, 6), position), (blocks,), jnp.float32, least / len(pieces), largest / len(pieces))
        return jnp.repeat(jnp.exp(steps), shape[position] // blocks).reshape((-1,) + (1,) * (len(shape) - position - 1))

    factor_of = one(*pieces[0])
    for cut in pieces[1:]:
        factor_of = factor_of * one(*cut)
    return factor_of


def noise(stream_key, dims, scale, limit, pieces=(), kind=jnp.bfloat16):
    values = jax.random.normal(stream_key, dims, jnp.float32) * scale
    if len(pieces) > 0:
        values = shard_levels(stream_key, dims, pieces, -0.22, 0.18) * values
    return jnp.clip(values, min=-limit, max=limit).astype(kind)


def setup_inputs(seed: int = 0) -> dict:
    keys = jax.random.split(jax.random.key(seed), 11)
    profiles = jnp.clip(0.5 + 1.5 * jax.random.uniform(keys[0], (2, PELLETS, NR), jnp.float32) ** shard_levels(keys[0], (2, PELLETS, NR), ((1, 256),), -0.2, 0.2), 0.5, 2.0)
    radial = draw_radial(jax.random.fold_in(keys[10], 71), 0)
    rate_const = jnp.clip(jnp.exp(math.log(0.2) - 2.3025851 * jax.random.uniform(keys[2], (PELLETS,), jnp.float32) ** shard_levels(keys[2], (PELLETS,), ((0, 256),), -0.2, 0.2)), 0.02, 0.2)
    transfer_coef = jnp.clip(jnp.exp(math.log(0.5) - 1.609438 * jax.random.uniform(keys[3], (PELLETS,), jnp.float32) ** shard_levels(keys[3], (PELLETS,), ((0, 256),), -0.2, 0.2)), 0.1, 0.5)
    live_count = draw_live_count(jax.random.fold_in(keys[10], 71), 0)
    send_lists = draw_send_lists(jax.random.fold_in(keys[10], 71), 0)
    cell_index = set_ends(jax.random.randint(keys[6], (PELLETS,), 0, CX * CY * NZ), jax.random.fold_in(keys[6], 1), 0, (CX * CY * NZ) - 1).astype(jnp.int32)
    contact_cols = draw_contact_cols(jax.random.fold_in(keys[10], 71), 0)
    contact_blocks = jnp.clip(0.006 * jax.random.uniform(keys[8], (N_GX * N_GY * PBLK, KB, BLK, BLK), jnp.float32) ** shard_levels(keys[8], (N_GX * N_GY * PBLK, KB, BLK, BLK), ((0, 256),), -0.2, 0.2), 0.0, 0.006)
    populations = noise(keys[9], (7, NX, NY, NZ), 0.3, 1.8, ((1, 16), (2, 16)), jnp.float32)
    return dict(profiles=profiles, radial=radial, rate_const=rate_const, transfer_coef=transfer_coef, live_count=live_count, send_lists=send_lists, cell_index=cell_index, contact_cols=contact_cols, contact_blocks=contact_blocks, populations=populations)


OFFSETS = ((-1, -1), (-1, 0), (-1, 1), (0, -1), (0, 1), (1, -1), (1, 0), (1, 1))
LATTICE_WEIGHTS = np.array([0.25, 0.125, 0.125, 0.125, 0.125, 0.125, 0.125], dtype=np.float32)


def shift_axis(values, amount, axis_number):
    if amount == 0:
        return values
    length = values.shape[axis_number]
    zeros_part = jnp.zeros_like(lax.slice_in_dim(values, 0, 1, axis=axis_number))
    if amount == 1:
        return jnp.concatenate([zeros_part, lax.slice_in_dim(values, 0, length - 1, axis=axis_number)], axis=axis_number)
    return jnp.concatenate([lax.slice_in_dim(values, 1, length, axis=axis_number), zeros_part], axis=axis_number)


def shift_grid(values, offset_x, offset_y):
    return shift_axis(shift_axis(values, offset_x, 0), offset_y, 1)


def stream_cells(post):
    padded = jnp.pad(post, ((0, 0), (1, 1), (1, 1), (1, 1)))
    return jnp.stack([
        padded[0, 1:-1, 1:-1, 1:-1],
        padded[1, :-2, 1:-1, 1:-1],
        padded[2, 2:, 1:-1, 1:-1],
        padded[3, 1:-1, :-2, 1:-1],
        padded[4, 1:-1, 2:, 1:-1],
        padded[5, 1:-1, 1:-1, :-2],
        padded[6, 1:-1, 1:-1, 2:],
    ])


def reference(profiles, radial, rate_const, transfer_coef, live_count, send_lists, cell_index, contact_cols, contact_blocks, populations):
    slots = PBLK * BLK
    tiles_x = N_GX
    tiles_y = N_GY
    total = slots * tiles_x * tiles_y
    weights = jnp.asarray(LATTICE_WEIGHTS).reshape(7, 1, 1, 1)
    live = (jnp.arange(slots, dtype=jnp.int32)[None, :] < live_count[:, None]).astype(jnp.float32).reshape(-1)
    ones_grid = jnp.ones((tiles_x, tiles_y), jnp.float32)
    exists = jnp.stack([shift_grid(ones_grid, pair[0], pair[1]) for pair in OFFSETS], axis=2)
    ghost_live = jnp.broadcast_to(exists[:, :, :, None], (tiles_x, tiles_y, 8, BLK)).reshape(tiles_x, tiles_y, 8 * BLK)
    live_ext = jnp.concatenate([live.reshape(tiles_x, tiles_y, slots), ghost_live], axis=2).reshape(tiles_x, tiles_y, PBLK + 8, BLK)
    lists = send_lists.reshape(tiles_x, tiles_y, 8, BLK)
    columns = contact_cols.reshape(tiles_x, tiles_y, PBLK, KB)
    blocks = contact_blocks.reshape(tiles_x, tiles_y, PBLK, KB, BLK, BLK)
    picker = jax.vmap(jax.vmap(lambda table, where_rows: table[where_rows]))
    tile_of = jnp.arange(total, dtype=jnp.int32) // slots
    tile_row = tile_of // tiles_y
    tile_col = tile_of % tiles_y
    local_x = cell_index // (CY * NZ)
    local_y = (cell_index // NZ) % CY
    local_z = cell_index % NZ
    global_cell = ((tile_row * CX + local_x) * (CY * tiles_y) + tile_col * CY + local_y) * NZ + local_z
    picked_live = picker(live_ext, columns)
    for turn_index in range(STEPS):
        temp = profiles[0]
        conc = profiles[1]
        theta = jnp.sum(populations, axis=0)
        shell = temp[:, NR - SHELL:]
        buffers = picker(shell.reshape(tiles_x, tiles_y, slots, SHELL), lists)
        ghosts = jnp.stack([shift_grid(buffers[:, :, number], OFFSETS[number][0], OFFSETS[number][1]) for number in range(8)], axis=2)
        own_rows = (shell * live[:, None]).reshape(tiles_x, tiles_y, slots, SHELL)
        extended = jnp.concatenate([own_rows, ghosts.reshape(tiles_x, tiles_y, 8 * BLK, SHELL)], axis=2).reshape(tiles_x, tiles_y, PBLK + 8, BLK, SHELL)
        picked = picker(extended, columns)
        flow = jnp.einsum("xyrkab,xyrkbs->xyras", blocks, picked, precision=lax.Precision.HIGHEST).reshape(total, SHELL)
        sink = jnp.einsum("xyrkab,xyrkb->xyra", blocks, picked_live, precision=lax.Precision.HIGHEST).reshape(total)
        contact = flow - sink[:, None] * shell
        theta_cell = theta.reshape(-1)[global_cell]
        exchange = transfer_coef * (theta_cell - temp[:, NR - 1]) * live
        rate = rate_const[:, None] * conc * jnp.exp(0.5 * jnp.tanh(temp - 1.0))
        mixed = jnp.einsum("cpj,cjk->cpk", profiles, radial, precision=lax.Precision.HIGHEST)
        new_temp = mixed[0] + rate
        new_temp = new_temp.at[:, NR - SHELL:].add(contact)
        new_temp = new_temp.at[:, NR - 1].add(exchange)
        new_conc = mixed[1] - rate
        updated = jnp.stack([new_temp, new_conc])
        profiles = jnp.where(live[None, :, None] > 0.0, updated, profiles)
        source = -0.5 * jax.ops.segment_sum(exchange, global_cell, num_segments=theta.size).reshape(theta.shape)
        post = populations - (populations - weights * theta[None]) / 0.8 + weights * source[None]
        populations = stream_cells(post)
    return profiles, populations
```

```python
import functools

import jax
import jax.numpy as jnp
from jax import lax
from jax.experimental import pallas as pl
from jax.experimental.pallas import tpu as pltpu
from jax.sharding import PartitionSpec as P

NR = 128
BLK = 128
SHELL = 16
STEPS = 3
PB = 8
SLOTS = PB * BLK
CX = 32
CELLS = 1024
F32 = jnp.float32
BF16 = jnp.bfloat16

OFFSETS = ((-1, -1), (-1, 0), (-1, 1), (0, -1), (0, 1), (1, -1), (1, 0), (1, 1))
NT = (((1,), (1,)), ((), ()))
NN = (((1,), (0,)), ((), ()))
VM = pl.BlockSpec(memory_space=pltpu.VMEM)
SM = pl.BlockSpec(memory_space=pltpu.SMEM)
ANY = pl.BlockSpec(memory_space=pl.ANY)
PARAMS = pltpu.CompilerParams(vmem_limit_bytes=30 * 1024 * 1024)


def dot(a, b, dims=NN):
    return lax.dot_general(a, b, dims, preferred_element_type=F32)


def split2(x):
    hi = x.astype(BF16)
    return hi, (x - hi.astype(F32)).astype(BF16)


def split3(x):
    hi = x.astype(BF16)
    rest = x - hi.astype(F32)
    mid = rest.astype(BF16)
    return hi, mid, (rest - mid.astype(F32)).astype(BF16)


def flag(cond):
    return jnp.where(cond, 1.0, 0.0).astype(F32)


def pair(ref, j):
    return jnp.concatenate([ref[2 * j : 2 * j + 1, :], ref[2 * j + 1 : 2 * j + 2, :]], axis=1)


def send_part(theta, edge, tt, cell, coef, blocks, ot, slt, thl, vt, source, ex, xu, xd, yu, yd):
    for b in range(PB):
        hi, lo = split2(theta[b * BLK : (b + 1) * BLK, :].T)
        thl[0:128, b * BLK : (b + 1) * BLK] = hi
        thl[128:256, b * BLK : (b + 1) * BLK] = lo
    sub = lax.broadcasted_iota(jnp.int32, (128, 256), 0)
    for j in range(4):
        at = slice(j * 256, (j + 1) * 256)
        g = dot(thl[...], ot[:, at])
        mask = sub == (pair(cell, j) & 127)
        there = jnp.sum(jnp.where(mask, g[0:128, :] + g[128:256, :], 0.0), axis=0, keepdims=True)
        alive = jnp.concatenate(
            [jnp.full((1, 128), flag(2 * j + h < blocks), F32) for h in range(2)], axis=1
        )
        e = pair(coef, j) * (there - tt[15:16, at]) * alive
        ex[2 * j : 2 * j + 1, :] = e[:, 0:128]
        ex[2 * j + 1 : 2 * j + 2, :] = e[:, 128:256]
        hi, lo = split2(jnp.where(mask, e, 0.0))
        vt[0:128, at] = hi
        vt[128:256, at] = lo
    for j in range(4):
        at = slice(j * 256, (j + 1) * 256)
        g = dot(ot[at, :], vt[...], NT)
        source[at, :] = 1.25 * theta[at, :] - 0.5 * (g[:, 0:128] + g[:, 128:256])
    xu[48:80, :] = 0.125 * source[992:1024, :] - 0.25 * edge[0]
    xd[48:80, :] = 0.125 * source[0:32, :] - 0.25 * edge[1]
    yu[16:48, :] = 0.125 * source[pl.ds(31, 32, stride=32), :] - 0.25 * edge[2]
    yd[16:48, :] = 0.125 * source[pl.ds(0, 32, stride=32), :] - 0.25 * edge[3]
    rows = jnp.concatenate(split3(tt[...]), axis=0)
    places = ((xd, 0), (xd, 16), (xd, 32), (yd, 0), (yu, 0), (xu, 0), (xu, 16), (xu, 32))
    for j in range(4):
        g = dot(rows, slt[:, j * 256 : (j + 1) * 256])
        g = g[0:16, :] + g[16:32, :] + g[32:48, :]
        for h in range(2):
            ref, start = places[2 * j + h]
            ref[start : start + 16, :] = g[:, h * 128 : (h + 1) * 128]


def first_kernel(
    live, cell, coef, lists, profiles, pops, ot, slt, tt, source, ex, xu, xd, yu, yd, theta, edge, thl, vt
):
    blocks = live[0] // BLK
    sub = lax.broadcasted_iota(jnp.int32, (CELLS, BLK), 0)
    for b in range(PB):
        at = slice(b * BLK, (b + 1) * BLK)
        ot[:, at] = jnp.where(sub == (cell[b : b + 1, :] >> 7), 1.0, 0.0).astype(BF16)
        slt[:, at] = jnp.where(sub == lists[b : b + 1, :], 1.0, 0.0).astype(BF16)
        tt[:, at] = profiles[0, at, :].T[NR - SHELL :, :]

    def row(x, _):
        at = pl.ds(pl.multiple_of(x * 32, 32), 32)
        total = pops[0, at, :]
        for i in range(1, 7):
            total = total + pops[i, at, :]
        theta[at, :] = total
        return 0

    lax.fori_loop(0, CX, row, 0)
    edge[0] = pops[1, 992:1024, :]
    edge[1] = pops[2, 0:32, :]
    edge[2] = pops[3, pl.ds(31, 32, stride=32), :]
    edge[3] = pops[4, pl.ds(0, 32, stride=32), :]
    send_part(theta, edge, tt, cell, coef, blocks, ot, slt, thl, vt, source, ex, xu, xd, yu, yd)


def stream_kernel(last, n_faces, *refs):
    faces, refs = refs[:n_faces], refs[n_faces:]
    if last:
        pops, source, new, strip3, strip4 = refs
    else:
        pops, source, new, theta, edge = refs
    y = lax.broadcasted_iota(jnp.int32, (32, 128), 0)
    z = lax.broadcasted_iota(jnp.int32, (32, 128), 1)

    def row(x, _):
        at = pl.ds(pl.multiple_of(x * 32, 32), 32)
        before = pl.ds(pl.multiple_of(jnp.maximum(x - 1, 0) * 32, 32), 32)
        after = pl.ds(pl.multiple_of(jnp.minimum(x + 1, CX - 1) * 32, 32), 32)
        s = 0.125 * source[at, :]
        n0 = 2.0 * s - 0.25 * pops[0, at, :]
        new[0, at, :] = n0
        n1 = flag(x > 0) * (0.125 * source[before, :] - 0.25 * pops[1, before, :])
        new[1, at, :] = n1
        n2 = flag(x < CX - 1) * (0.125 * source[after, :] - 0.25 * pops[2, after, :])
        new[2, at, :] = n2
        n3 = jnp.where(y == 0, 0.0, pltpu.roll(s - 0.25 * pops[3, at, :], 1, 0))
        new[3, at, :] = n3
        n4 = jnp.where(y == 31, 0.0, pltpu.roll(s - 0.25 * pops[4, at, :], 31, 0))
        new[4, at, :] = n4
        n5 = jnp.where(z == 0, 0.0, pltpu.roll(s - 0.25 * pops[5, at, :], 1, 1))
        new[5, at, :] = n5
        n6 = jnp.where(z == 127, 0.0, pltpu.roll(s - 0.25 * pops[6, at, :], 127, 1))
        new[6, at, :] = n6
        if not last:
            theta[at, :] = ((n0 + n1) + (n2 + n3)) + ((n4 + n5) + n6)
        return 0

    lax.fori_loop(0, CX, row, 0, unroll=2)
    if n_faces:
        meta, xu, xd, yu, yd = faces
        parts = (
            (1, slice(32, 64), 6, xu[48:80, :]),
            (2, slice(960, 992), 1, xd[48:80, :]),
            (3, pl.ds(1, 32, stride=32), 4, yu[16:48, :]),
            (4, pl.ds(30, 32, stride=32), 3, yd[16:48, :]),
        )
        for i, at, place, face in parts:
            face = face * (-0.25 * meta[place].astype(F32))
            new[i, at, :] = new[i, at, :] + face
            if not last:
                theta[at, :] = theta[at, :] + face
    if last:
        for x in range(CX):
            strip3[x] = new[3, x * 32 : x * 32 + 8, :]
            strip4[x] = new[4, x * 32 + 24 : x * 32 + 32, :]
    else:
        edge[0] = new[1, 992:1024, :]
        edge[1] = new[2, 0:32, :]
        edge[2] = new[3, pl.ds(31, 32, stride=32), :]
        edge[3] = new[4, pl.ds(0, 32, stride=32), :]


def prepare_kernel(rate, blocks, rc, halves):
    for b in range(PB):
        rc[b * BLK : (b + 1) * BLK, :] = jnp.broadcast_to(rate[b : b + 1, :], (BLK, NR)).T
        for k in range(4):
            hi, lo = split2(blocks[b, k])
            halves[b, k, :, 0:128] = hi
            halves[b, k, :, 128:256] = lo


def mix_part(blocks, temp_of, conc_of, radial, rc, base, conc_new):
    wide = []
    for c in range(2):
        hi, lo = split2(radial[c])
        wide.append(
            jnp.concatenate(
                [jnp.concatenate([hi, lo], axis=1), jnp.concatenate([hi, jnp.zeros_like(hi)], axis=1)],
                axis=0,
            )
        )
    for b in range(PB):
        at = slice(b * BLK, (b + 1) * BLK)
        temp, conc = temp_of(at), conc_of(at)
        alive = flag(b < blocks)
        rate = rc[at, :] * conc * jnp.exp(0.5 * jnp.tanh(temp - 1.0))
        g = dot(jnp.concatenate(split2(temp), axis=1), wide[0])
        base[at, :] = (g[:, 0:128] + g[:, 128:256]) + rate
        g = dot(jnp.concatenate(split2(conc), axis=1), wide[1])
        conc_new[at, :] = alive * ((g[:, 0:128] + g[:, 128:256]) - rate) + (1.0 - alive) * conc


def mix_first_kernel(live, profiles, radial, rc, base, conc_new):
    mix_part(live[0] // BLK, lambda at: profiles[0, at, :], lambda at: profiles[1, at, :], radial, rc, base, conc_new)


def mix_kernel(live, temp, conc, radial, rc, base, conc_new):
    mix_part(live[0] // BLK, lambda at: temp[at, :], lambda at: conc[at, :], radial, rc, base, conc_new)


def contact_part(live_blocks, meta, cols, temp_of, base, ex, tt, halves, rxu, rxd, ryu, ryd, extended, store):
    for b in range(PB):
        alive = flag(b < live_blocks)
        hi, lo = split2(tt[:, b * BLK : (b + 1) * BLK] * alive)
        extended[b, 0:16, :] = hi
        extended[b, 16:32, :] = lo
        extended[b, 32:48, :] = jnp.full((16, 128), alive, F32).astype(BF16)
    places = ((ryd, 48), (rxd, 16), (ryu, 48), (ryd, 0), (ryu, 0), (ryd, 64), (rxu, 16), (ryu, 64))
    for n in range(8):
        ref, start = places[n]
        there = meta[n].astype(F32)
        hi, lo = split2(ref[start : start + 16, :] * there)
        extended[8 + n, 0:16, :] = hi
        extended[8 + n, 16:32, :] = lo
        extended[8 + n, 32:48, :] = jnp.full((16, 128), there, F32).astype(BF16)
    row = lax.broadcasted_iota(jnp.int32, (16, 128), 0)
    for b in range(PB):
        at = slice(b * BLK, (b + 1) * BLK)
        total = None
        for k in range(4):
            x = extended[cols[b, k]]
            g = dot(jnp.concatenate([x, x], axis=1), halves[b, k], NT)
            total = g if total is None else total + g
        flow = total[0:16, :] + total[16:32, :] - total[32:33, :] * tt[:, at]
        flow = jnp.where(row == 15, flow + ex[b : b + 1, :], flow)
        added = jnp.concatenate([jnp.zeros((NR - SHELL, BLK), F32), flow], axis=0).T
        alive = flag(b < live_blocks)
        store(b, at, alive * (base[at, :] + added) + (1.0 - alive) * temp_of(at))


def middle_kernel(
    temp_3d, live, meta, cols, temp, base, ex_in, tt_in, halves, rxu, rxd, ryu, ryd,
    theta_in, edge, cell, coef, ot, slt,
    temp_out, tt, source, ex, xu, xd, yu, yd, extended, theta, thl, vt,
):
    blocks = live[0] // BLK

    def store(b, at, value):
        temp_out[at, :] = value
        tt[:, at] = value.T[NR - SHELL :, :]

    old = (lambda at: temp[0, at, :]) if temp_3d else (lambda at: temp[at, :])
    contact_part(blocks, meta, cols, old, base, ex_in, tt_in, halves, rxu, rxd, ryu, ryd, extended, store)
    theta[...] = theta_in[...]
    for at, place, face in (
        (slice(0, 32), 6, rxu[48:80, :]),
        (slice(992, 1024), 1, rxd[48:80, :]),
        (pl.ds(0, 32, stride=32), 4, ryu[16:48, :]),
        (pl.ds(31, 32, stride=32), 3, ryd[16:48, :]),
    ):
        theta[at, :] = theta[at, :] + face * meta[place].astype(F32)
    send_part(theta, edge, tt, cell, coef, blocks, ot, slt, thl, vt, source, ex, xu, xd, yu, yd)


def last_kernel(
    live, meta, cols, temp, base, conc, ex_in, tt_in, halves, rxu, rxd, ryu, ryd, strip3, strip4, pops_in,
    profiles, pops, extended, face1, face2, patch3, patch4, sems,
):
    face1[...] = rxu[48:80, :] * meta[6].astype(F32)
    face2[...] = rxd[48:80, :] * meta[1].astype(F32)
    y = lax.broadcasted_iota(jnp.int32, (8, 128), 0)
    for x in range(CX):
        patch3[x] = jnp.where(y == 0, ryu[16 + x : 17 + x, :] * meta[4].astype(F32), strip3[x])
        patch4[x] = jnp.where(y == 7, ryd[16 + x : 17 + x, :] * meta[3].astype(F32), strip4[x])
    copies = [
        pltpu.make_async_copy(face1, pops.at[1, 0], sems.at[0]),
        pltpu.make_async_copy(face2, pops.at[2, CX - 1], sems.at[1]),
        pltpu.make_async_copy(patch3, pops.at[3, :, 0:8, :], sems.at[2]),
        pltpu.make_async_copy(patch4, pops.at[4, :, 24:32, :], sems.at[3]),
    ]
    for c in copies:
        c.start()

    def store(b, at, value):
        profiles[0, at, :] = value
        profiles[1, at, :] = conc[at, :]

    old = lambda at: temp[at, :]
    contact_part(
        live[0] // BLK, meta, cols, old, base, ex_in, tt_in, halves, rxu, rxd, ryu, ryd, extended, store
    )
    for c in copies:
        c.wait()


def call(kernel, name, ins, in_specs, outs, out_specs=None, scratch=(), us=2, aliases=None):
    shapes = [jax.ShapeDtypeStruct(s, d) for s, d in outs]
    return pl.pallas_call(
        kernel,
        name=name,
        out_shape=shapes,
        in_specs=in_specs,
        out_specs=[VM] * len(outs) if out_specs is None else out_specs,
        scratch_shapes=list(scratch),
        compiler_params=PARAMS,
        input_output_aliases=aliases or {},
        cost_estimate=pl.CostEstimate(flops=us * 10**8, bytes_accessed=us * 3 * 10**6, transcendentals=0),
    )(*ins)


def exchange_x(xu, xd):
    n = lax.axis_size("gx")
    up = [(i, (i + 1) % n) for i in range(n)]
    down = [(j, i) for i, j in up]
    return lax.ppermute(xu, "gx", up), lax.ppermute(xd, "gx", down)


def exchange_y(yu, yd, rxu, rxd):
    n = lax.axis_size("gy")
    up = [(i, (i + 1) % n) for i in range(n)]
    down = [(j, i) for i, j in up]
    to_up = jnp.concatenate([yu, rxd[32:48], rxu[32:48]], axis=0)
    to_down = jnp.concatenate([yd, rxd[0:16], rxu[0:16]], axis=0)
    return lax.ppermute(to_up, "gy", up), lax.ppermute(to_down, "gy", down)


def on_device(
    profiles, radial, rate_const, transfer_coef, live_count, send_lists, cell_index, contact_cols, contact_blocks, populations
):
    cell = cell_index.reshape(PB, BLK)
    coef = transfer_coef.reshape(PB, BLK)
    rate = rate_const.reshape(PB, BLK)
    pops = populations.reshape(7, CELLS, 128)
    blocks = contact_blocks.reshape(PB, 4, BLK, BLK)
    ix, iy = lax.axis_index("gx"), lax.axis_index("gy")
    nx, ny = lax.axis_size("gx"), lax.axis_size("gy")
    meta = jnp.stack(
        [
            ((ix - a >= 0) & (ix - a < nx) & (iy - b >= 0) & (iy - b < ny)).astype(jnp.int32)
            for a, b in OFFSETS
        ]
    )
    plane = ((SLOTS, 128), F32)
    out_send = [((80, 128), F32)] * 2 + [((48, 128), F32)] * 2
    work = [pltpu.VMEM((256, 1024), BF16), pltpu.VMEM((256, 1024), BF16)]
    theta_s = pltpu.VMEM((CELLS, 128), F32)
    ext_s = pltpu.VMEM((16, 48, 128), BF16)

    ot, slt, tt, source, ex, xu, xd, yu, yd = call(
        first_kernel, "first",
        (live_count, cell, coef, send_lists, profiles, pops), [SM] + [VM] * 5,
        [((CELLS, SLOTS), BF16), ((SLOTS, SLOTS), BF16), ((SHELL, SLOTS), F32), plane, ((PB, BLK), F32)] + out_send,
        scratch=[theta_s, pltpu.VMEM((4, 32, 128), F32)] + work, us=6,
    )
    rc, halves = call(
        prepare_kernel, "prepare", (rate, blocks), [VM, VM], [plane, ((PB, 4, BLK, 256), BF16)]
    )
    temp = conc = received = None
    for step in range(STEPS):
        final = step == STEPS - 1
        rxu, rxd = exchange_x(xu, xd)
        if step == 0:
            base, conc_new = call(
                mix_first_kernel, "mix_first", (live_count, profiles, radial, rc), [SM] + [VM] * 3, [plane, plane]
            )
        else:
            base, conc_new = call(
                mix_kernel, "mix", (live_count, temp, conc, radial, rc), [SM] + [VM] * 4, [plane, plane]
            )
        faces = () if step == 0 else (meta, *received)
        last_outs = [((CX, 8, 128), F32)] * 2 if final else [plane, ((4, 32, 128), F32)]
        streamed = call(
            functools.partial(stream_kernel, final, len(faces)), "stream",
            (*faces, pops, source), [SM] * (step > 0) + [VM] * (6 if step else 2),
            [((7, CELLS, 128), F32)] + last_outs,
        )
        ryu, ryd = exchange_y(yu, yd, rxu, rxd)
        received = (rxu, rxd, ryu, ryd)
        if final:
            whole = streamed[0].reshape(7, CX, 32, 128)
            profiles_out, pops_out = call(
                last_kernel, "last",
                (live_count, meta, contact_cols, temp, base, conc_new, ex, tt, halves, *received, *streamed[1:], whole),
                [SM] * 3 + [VM] * 12 + [ANY],
                [((2, SLOTS, NR), F32), ((7, CX, 32, 128), F32)],
                out_specs=[VM, ANY],
                scratch=[ext_s] + [pltpu.VMEM((32, 128), F32)] * 2 + [pltpu.VMEM((CX, 8, 128), F32)] * 2
                + [pltpu.SemaphoreType.DMA((4,))],
                aliases={15: 1},
            )
            return profiles_out, pops_out
        pops, theta, edge = streamed
        temp, tt, source, ex, xu, xd, yu, yd = call(
            functools.partial(middle_kernel, step == 0), "middle",
            (live_count, meta, contact_cols, profiles if step == 0 else temp, base, ex, tt, halves, *received,
             theta, edge, cell, coef, ot, slt),
            [SM] * 3 + [VM] * 15,
            [plane, ((SHELL, SLOTS), F32), plane, ((PB, BLK), F32)] + out_send,
            scratch=[ext_s, theta_s] + work, us=6,
        )
        conc = conc_new


def solution(mesh):
    return jax.shard_map(
        on_device,
        mesh=mesh,
        in_specs=(
            P(None, ("gx", "gy"), None),
            P(),
            P(("gx", "gy")),
            P(("gx", "gy")),
            P(("gx", "gy")),
            P(("gx", "gy"), None),
            P(("gx", "gy")),
            P(("gx", "gy"), None),
            P(("gx", "gy"), None, None, None),
            P(None, "gx", "gy", None),
        ),
        out_specs=(P(None, ("gx", "gy"), None), P(None, "gx", "gy", None)),
        check_vma=False,
    )
```

```python
import functools

import jax
import jax.numpy as jnp
from jax import lax
from jax.experimental import pallas as pl
from jax.experimental.pallas import tpu as pltpu
from jax.sharding import PartitionSpec as P

NR = 128
BLK = 128
SHELL = 16
STEPS = 3
PB = 8
SLOTS = PB * BLK
CX = 32
CELLS = 1024
CHUNKS = 4
CHUNK = CELLS // CHUNKS
F32 = jnp.float32
BF16 = jnp.bfloat16

OFFSETS = ((-1, -1), (-1, 0), (-1, 1), (0, -1), (0, 1), (1, -1), (1, 0), (1, 1))
NT = (((1,), (1,)), ((), ()))
NN = (((1,), (0,)), ((), ()))
VM = pl.BlockSpec(memory_space=pltpu.VMEM)
SM = pl.BlockSpec(memory_space=pltpu.SMEM)
HBM = pl.BlockSpec(memory_space=pltpu.HBM)

FACES = (slice(992, 1024), slice(0, 32), pl.ds(31, 32, stride=32), pl.ds(0, 32, stride=32))


def dot(a, b, dims=NN):
    return lax.dot_general(a, b, dims, preferred_element_type=F32)


def split2(x):
    hi = x.astype(BF16)
    return hi, (x - hi.astype(F32)).astype(BF16)


def split3(x):
    hi = x.astype(BF16)
    rest = x - hi.astype(F32)
    mid = rest.astype(BF16)
    return hi, mid, (rest - mid.astype(F32)).astype(BF16)


def flag(cond):
    return jnp.where(cond, 1.0, 0.0).astype(F32)


def neighbour(n):
    a, b = OFFSETS[n]
    x, y = lax.axis_index("gx") - a, lax.axis_index("gy") - b
    return flag((x >= 0) & (x < lax.axis_size("gx")) & (y >= 0) & (y < lax.axis_size("gy")))


def halves_of(g):
    return g[:, 0:128] + g[:, 128:256]


def pair(ref, j):
    return jnp.concatenate([ref[2 * j : 2 * j + 1, :], ref[2 * j + 1 : 2 * j + 2, :]], axis=1)


def store_pair(ref, j, row):
    ref[2 * j : 2 * j + 1, :] = row[:, 0:128]
    ref[2 * j + 1 : 2 * j + 2, :] = row[:, 128:256]


def lane_mask(cell, j):
    return lax.broadcasted_iota(jnp.int32, (128, 256), 0) == (pair(cell, j) & 127)


def pick(mask, g):
    return jnp.sum(jnp.where(mask, g[0:128, :] + g[128:256, :], 0.0), axis=0, keepdims=True)


def send_ghosts(tt, slt, xu, xd, yu, yd):
    rows = jnp.concatenate(split3(tt[...]), axis=0)
    places = ((xd, 0), (xd, 16), (xd, 32), (yd, 0), (yu, 0), (xu, 0), (xu, 16), (xu, 32))
    for j in range(4):
        g = dot(rows, slt[:, j * 256 : (j + 1) * 256])
        g = g[0:16, :] + g[16:32, :] + g[32:48, :]
        for h in range(2):
            ref, start = places[2 * j + h]
            ref[start : start + 16, :] = g[:, h * 128 : (h + 1) * 128]


def send_faces(there, theta, edge, tt, cell, coef, blocks, otf, ex, vt, xu, xd, yu, yd):
    for j in range(4):
        at = slice(j * 256, (j + 1) * 256)
        alive = jnp.concatenate(
            [jnp.full((1, 128), flag(2 * j + h < blocks), F32) for h in range(2)], axis=1
        )
        e = pair(coef, j) * (there[j] - tt[15:16, at]) * alive
        store_pair(ex, j, e)
        hi, lo = split2(jnp.where(lane_mask(cell, j), e, 0.0))
        vt[0:128, at] = hi
        vt[128:256, at] = lo
    source = halves_of(dot(otf[...], vt[...], NT))
    outs = ((xu, 48), (xd, 48), (yu, 16), (yd, 16))
    for f in range(4):
        ref, start = outs[f]
        rows = slice(f * 32, (f + 1) * 32)
        s = 1.25 * theta[FACES[f], :] - 0.5 * source[rows, :]
        ref[start : start + 32, :] = 0.125 * s - 0.25 * edge[rows, :]


def first_kernel(
    live, cell_in, coef_in, lists_in, prof_in, pops_in,
    cell, coef, prof, pops, ot, slt, otf, tt, theta, ex, vt, xu, xd, yu, yd,
    lists, gathered, edge, sems,
):
    blocks = live[0] // BLK
    copies = [
        pltpu.make_async_copy(cell_in, cell, sems.at[0]),
        pltpu.make_async_copy(lists_in, lists, sems.at[1]),
        pltpu.make_async_copy(prof_in.at[0], prof.at[0], sems.at[2]),
    ]
    for c in range(CHUNKS):
        rows = pl.ds(c * CHUNK, CHUNK)
        copies.append(pltpu.make_async_copy(pops_in.at[:, rows, :], pops.at[:, rows, :], sems.at[3 + c]))
    copies.append(pltpu.make_async_copy(coef_in, coef, sems.at[3 + CHUNKS]))
    copies.append(pltpu.make_async_copy(prof_in.at[1], prof.at[1], sems.at[4 + CHUNKS]))
    for c in copies:
        c.start()
    sub = lax.broadcasted_iota(jnp.int32, (CELLS, BLK), 0)
    f = lax.broadcasted_iota(jnp.int32, (128, BLK), 0)
    f_row = jnp.where(f < 32, f + 992, jnp.where(f < 64, f - 32, jnp.where(f < 96, f * 32 - 2017, f * 32 - 3072)))
    copies[0].wait()
    for b in range(PB):
        at = slice(b * BLK, (b + 1) * BLK)
        row = cell[b : b + 1, :] >> 7
        ot[:, at] = jnp.where(sub == row, 1.0, 0.0).astype(BF16)
        otf[:, at] = jnp.where(f_row == row, 1.0, 0.0).astype(BF16)
    copies[1].wait()
    for b in range(PB):
        at = slice(b * BLK, (b + 1) * BLK)
        slt[:, at] = jnp.where(sub == lists[b : b + 1, :], 1.0, 0.0).astype(BF16)
    copies[2].wait()
    for b in range(PB):
        at = slice(b * BLK, (b + 1) * BLK)
        tt[:, at] = prof[0, at, :].T[NR - SHELL :, :]
    send_ghosts(tt, slt, xu, xd, yu, yd)
    for c in range(CHUNKS):
        copies[3 + c].wait()
        parts = []
        for h in range(CHUNK // 128):
            at = slice(c * CHUNK + h * 128, c * CHUNK + (h + 1) * 128)
            total = pops[0, at, :]
            for i in range(1, 7):
                total = total + pops[i, at, :]
            theta[at, :] = total
            parts.append(jnp.concatenate(split2(total.T), axis=0))
        rows = jnp.concatenate(parts, axis=1)
        for j in range(4):
            at = slice(j * 256, (j + 1) * 256)
            g = dot(rows, ot[c * CHUNK : (c + 1) * CHUNK, at])
            gathered[:, at] = g if c == 0 else gathered[:, at] + g
    for i in range(4):
        edge[i * 32 : (i + 1) * 32, :] = pops[i + 1, FACES[i], :]
    copies[3 + CHUNKS].wait()
    there = [pick(lane_mask(cell, j), gathered[:, j * 256 : (j + 1) * 256]) for j in range(4)]
    send_faces(there, theta, edge, tt, cell, coef, blocks, otf, ex, vt, xu, xd, yu, yd)
    copies[4 + CHUNKS].wait()


def stream_kernel(last, has_faces, *refs):
    if has_faces:
        faces, refs = refs[0], refs[1:]
    if last:
        pops, theta, vt, ot, out, strip3, strip4, source, new, sems = refs
    else:
        pops, theta, vt, ot, cell, new, theta_new, edge, there, source, rows = refs
    for j in range(4):
        at = slice(j * 256, (j + 1) * 256)
        source[at, :] = 1.25 * theta[at, :] - 0.5 * halves_of(dot(ot[at, :], vt[...], NT))
    y = lax.broadcasted_iota(jnp.int32, (32, 128), 0)
    z = lax.broadcasted_iota(jnp.int32, (32, 128), 1)

    def row(x, _):
        at = pl.ds(pl.multiple_of(x * 32, 32), 32)
        before = pl.ds(pl.multiple_of(jnp.maximum(x - 1, 0) * 32, 32), 32)
        after = pl.ds(pl.multiple_of(jnp.minimum(x + 1, CX - 1) * 32, 32), 32)
        s = 0.125 * source[at, :]
        n0 = 2.0 * s - 0.25 * pops[0, at, :]
        new[0, at, :] = n0
        n1 = flag(x > 0) * (0.125 * source[before, :] - 0.25 * pops[1, before, :])
        new[1, at, :] = n1
        n2 = flag(x < CX - 1) * (0.125 * source[after, :] - 0.25 * pops[2, after, :])
        new[2, at, :] = n2
        n3 = jnp.where(y == 0, 0.0, pltpu.roll(s - 0.25 * pops[3, at, :], 1, 0))
        new[3, at, :] = n3
        n4 = jnp.where(y == 31, 0.0, pltpu.roll(s - 0.25 * pops[4, at, :], 31, 0))
        new[4, at, :] = n4
        n5 = jnp.where(z == 0, 0.0, pltpu.roll(s - 0.25 * pops[5, at, :], 1, 1))
        new[5, at, :] = n5
        n6 = jnp.where(z == 127, 0.0, pltpu.roll(s - 0.25 * pops[6, at, :], 127, 1))
        new[6, at, :] = n6
        if not last:
            theta_new[at, :] = ((n0 + n1) + (n2 + n3)) + ((n4 + n5) + n6)
        return 0

    def carry_faces(c):
        parts = (
            (0, 1, slice(32, 64), faces[32:64, :]),
            (CHUNKS - 1, 2, slice(960, 992), faces[0:32, :]),
            (c, 3, pl.ds(c * CHUNK + 1, 8, stride=32), faces[96 + c * 8 : 104 + c * 8, :]),
            (c, 4, pl.ds(c * CHUNK + 30, 8, stride=32), faces[64 + c * 8 : 72 + c * 8, :]),
        )
        for chunk, i, at, face in parts:
            if chunk == c:
                new[i, at, :] = new[i, at, :] - 0.25 * face
                if not last:
                    theta_new[at, :] = theta_new[at, :] - 0.25 * face

    copies = []
    for c in range(CHUNKS):
        lax.fori_loop(c * 8, (c + 1) * 8, row, 0, unroll=2)
        if has_faces:
            carry_faces(c)
        if last:
            at = pl.ds(c * CHUNK, CHUNK)
            copies.append(pltpu.make_async_copy(new.at[:, at, :], out.at[:, at, :], sems.at[c]))
            copies[-1].start()
            for x in range(c * 8, (c + 1) * 8):
                strip3[x] = new[3, x * 32 : x * 32 + 8, :]
                strip4[x] = new[4, x * 32 + 24 : x * 32 + 32, :]
    if last:
        for copy in copies:
            copy.wait()
        return
    for b in range(PB):
        at = slice(b * BLK, (b + 1) * BLK)
        hi, lo = split2(theta_new[at, :].T)
        rows[0:128, at] = hi
        rows[128:256, at] = lo
    for j in range(4):
        store_pair(there, j, pick(lane_mask(cell, j), dot(rows[...], ot[:, j * 256 : (j + 1) * 256])))
    for i in range(4):
        edge[i * 32 : (i + 1) * 32, :] = new[i + 1, FACES[i], :]


def prepare_kernel(rate, blocks, rc, halves):
    for b in range(PB):
        rc[b * BLK : (b + 1) * BLK, :] = jnp.broadcast_to(rate[b : b + 1, :], (BLK, NR)).T
        for k in range(4):
            hi, lo = split2(blocks[b, k])
            halves[b, k, :, 0:128] = hi
            halves[b, k, :, 128:256] = lo


def temp_now(b, at, blocks, prof, base, flow):
    added = jnp.concatenate([jnp.zeros((NR - SHELL, BLK), F32), flow[:, at]], axis=0).T
    alive = flag(b < blocks)
    return alive * (base[at, :] + added) + (1.0 - alive) * prof[0, at, :]


def mix_kernel(first, last, *refs):
    if first:
        live, prof, radial, rc, *refs = refs
    else:
        live, prof, radial, rc, base_in, flow, conc_in, *refs = refs
    if last:
        base, out, conc_new, sems = refs
    else:
        base, ttb, conc_new = refs
    blocks = live[0] // BLK
    wide = []
    for c in range(2):
        hi, lo = split2(radial[c])
        top = jnp.concatenate([hi, lo], axis=1)
        wide.append(jnp.concatenate([top, jnp.concatenate([hi, jnp.zeros_like(hi)], axis=1)], axis=0))
    copies = []
    for b in range(PB):
        at = slice(b * BLK, (b + 1) * BLK)
        conc = prof[1, at, :] if first else conc_in[at, :]
        temp = prof[0, at, :] if first else temp_now(b, at, blocks, prof, base_in, flow)
        alive = flag(b < blocks)
        rate = rc[at, :] * conc * jnp.exp(0.5 * jnp.tanh(temp - 1.0))
        value = halves_of(dot(jnp.concatenate(split2(temp), axis=1), wide[0])) + rate
        base[at, :] = value
        if not last:
            ttb[:, at] = value.T[NR - SHELL :, :]
        value = halves_of(dot(jnp.concatenate(split2(conc), axis=1), wide[1])) - rate
        conc_new[at, :] = alive * value + (1.0 - alive) * conc
        if last and b % 2 == 1:
            two = pl.ds((b - 1) * BLK, 2 * BLK)
            copies.append(pltpu.make_async_copy(conc_new.at[two, :], out.at[1, two, :], sems.at[b // 2]))
            copies[-1].start()
    for copy in copies:
        copy.wait()


def contact_part(blocks, cols, ex, tt, halves, rxu, rxd, ryu, ryd, extended, store):
    for b in range(PB):
        alive = flag(b < blocks)
        hi, lo = split2(tt[:, b * BLK : (b + 1) * BLK] * alive)
        extended[b, 0:16, :] = hi
        extended[b, 16:32, :] = lo
        extended[b, 32:48, :] = jnp.full((16, 128), alive, F32).astype(BF16)
    places = ((ryd, 48), (rxd, 16), (ryu, 48), (ryd, 0), (ryu, 0), (ryd, 64), (rxu, 16), (ryu, 64))
    for n in range(8):
        ref, start = places[n]
        there = neighbour(n)
        hi, lo = split2(ref[start : start + 16, :] * there)
        extended[8 + n, 0:16, :] = hi
        extended[8 + n, 16:32, :] = lo
        extended[8 + n, 32:48, :] = jnp.full((16, 128), there, F32).astype(BF16)
    row = lax.broadcasted_iota(jnp.int32, (16, 128), 0)
    for b in range(PB):
        at = slice(b * BLK, (b + 1) * BLK)
        total = None
        for k in range(4):
            x = extended[cols[k, b]]
            g = dot(jnp.concatenate([x, x], axis=1), halves[b, k], NT)
            total = g if total is None else total + g
        flow = total[0:16, :] + total[16:32, :] - total[32:33, :] * tt[:, at]
        store(b, at, jnp.where(row == 15, flow + ex[b : b + 1, :], flow))


def middle_kernel(
    live, cols, ex_in, tt_in, ttb, halves, rxu, rxd, ryu, ryd, theta_in, there_in, edge, cell, coef, otf, slt,
    flow, tt, theta, faces, ex, vt, xu, xd, yu, yd, extended,
):
    blocks = live[0] // BLK

    def store(b, at, value):
        flow[:, at] = value
        alive = flag(b < blocks)
        tt[:, at] = alive * (ttb[:, at] + value) + (1.0 - alive) * tt_in[:, at]

    contact_part(blocks, cols, ex_in, tt_in, halves, rxu, rxd, ryu, ryd, extended, store)
    send_ghosts(tt, slt, xu, xd, yu, yd)
    theta[...] = theta_in[...]
    came = ((rxd, 48, 1), (rxu, 48, 6), (ryd, 16, 3), (ryu, 16, 4))
    for f in range(4):
        ref, start, n = came[f]
        face = ref[start : start + 32, :] * neighbour(n)
        faces[f * 32 : (f + 1) * 32, :] = face
        theta[FACES[f], :] = theta[FACES[f], :] + face
    rows = jnp.concatenate(split2(faces[...].T), axis=0)
    there = []
    for j in range(4):
        more = pick(lane_mask(cell, j), dot(rows, otf[:, j * 256 : (j + 1) * 256]))
        there.append(pair(there_in, j) + more)
    send_faces(there, theta, edge, tt, cell, coef, blocks, otf, ex, vt, xu, xd, yu, yd)


def last_kernel(
    live, cols, prof, base, ex, tt, halves, rxu, rxd, ryu, ryd, strip3, strip4, prof_in, pops_in,
    profiles, pops, extended, flow, temp, face1, face2, patch3, patch4, sems,
):
    blocks = live[0] // BLK
    face1[...] = rxu[48:80, :] * neighbour(6)
    face2[...] = rxd[48:80, :] * neighbour(1)
    y = lax.broadcasted_iota(jnp.int32, (8, 128), 0)
    for x in range(CX):
        patch3[x] = jnp.where(y == 0, ryu[16 + x : 17 + x, :] * neighbour(4), strip3[x])
        patch4[x] = jnp.where(y == 7, ryd[16 + x : 17 + x, :] * neighbour(3), strip4[x])
    copies = [
        pltpu.make_async_copy(face1, pops.at[1, 0], sems.at[0]),
        pltpu.make_async_copy(face2, pops.at[2, CX - 1], sems.at[1]),
        pltpu.make_async_copy(patch3, pops.at[3, :, 0:8, :], sems.at[2]),
        pltpu.make_async_copy(patch4, pops.at[4, :, 24:32, :], sems.at[3]),
    ]
    for c in copies:
        c.start()

    def store(b, at, value):
        flow[:, at] = value
        temp[at, :] = temp_now(b, at, blocks, prof, base, flow)
        if b % 2 == 1:
            two = pl.ds((b - 1) * BLK, 2 * BLK)
            copies.append(pltpu.make_async_copy(temp.at[two, :], profiles.at[0, two, :], sems.at[4 + b // 2]))
            copies[-1].start()

    contact_part(blocks, cols, ex, tt, halves, rxu, rxd, ryu, ryd, extended, store)
    for c in copies:
        c.wait()


def call(kernel, name, ins, in_specs, outs, out_specs=None, scratch=(), us=2, aliases=None, mib=8):
    shapes = [jax.ShapeDtypeStruct(s, d) for s, d in outs]
    return pl.pallas_call(
        kernel,
        name=name,
        out_shape=shapes,
        in_specs=in_specs,
        out_specs=[VM] * len(outs) if out_specs is None else out_specs,
        scratch_shapes=list(scratch),
        compiler_params=pltpu.CompilerParams(vmem_limit_bytes=mib * 1024 * 1024),
        input_output_aliases=aliases or {},
        cost_estimate=pl.CostEstimate(flops=us * 10**8, bytes_accessed=us * 3 * 10**6, transcendentals=0),
    )(*ins)


def exchange(axis, to_up, to_down):
    n = lax.axis_size(axis)
    up = [(i, (i + 1) % n) for i in range(n)]
    down = [(j, i) for i, j in up]
    return lax.ppermute(to_up, axis, up), lax.ppermute(to_down, axis, down)


def on_device(
    profiles, radial, rate_const, transfer_coef, live_count, send_lists, cell_index, contact_cols, contact_blocks, populations
):
    blocks = contact_blocks.reshape(PB, 4, BLK, BLK)
    rate = rate_const.reshape(PB, BLK)
    cols = contact_cols.T
    plane, lanes, shells, square = ((SLOTS, 128), F32), ((PB, BLK), F32), ((SHELL, SLOTS), F32), ((128, 128), F32)
    lattice = ((7, CELLS, 128), F32)
    wide = ((256, 1024), BF16)
    sends = [((80, 128), F32)] * 2 + [((48, 128), F32)] * 2
    ext_s = pltpu.VMEM((16, 48, 128), BF16)

    stay = [
        pltpu.with_memory_space_constraint(a, pltpu.HBM)
        for a in (
            cell_index.reshape(PB, BLK),
            transfer_coef.reshape(PB, BLK),
            send_lists,
            profiles,
            populations.reshape(7, CELLS, 128),
        )
    ]
    cell, coef, prof, pops, ot, slt, otf, tt, theta, ex, vt, xu, xd, yu, yd = call(
        first_kernel, "first", (live_count, *stay),
        [SM] + [HBM] * 5,
        [((PB, BLK), jnp.int32), lanes, ((2, SLOTS, NR), F32), lattice, ((CELLS, SLOTS), BF16), ((SLOTS, SLOTS), BF16),
         ((128, SLOTS), BF16), shells, plane, lanes, wide] + sends,
        scratch=[pltpu.VMEM((PB, BLK), jnp.int32), pltpu.VMEM((256, 1024), F32), pltpu.VMEM((128, 128), F32),
                 pltpu.SemaphoreType.DMA((5 + CHUNKS,))],
        us=6,
    )
    faces = base = flow = conc = there = edge = None
    for step in range(STEPS):
        final = step == STEPS - 1
        rxu, rxd = exchange("gx", xu, xd)
        inputs = (() if step == 0 else (faces,)) + (pops, theta, vt, ot) + (() if final else (cell,))
        if final:
            outs, specs = [lattice] + [((CX, 8, 128), F32)] * 2, [HBM, VM, VM]
            scratch = [pltpu.VMEM(*plane), pltpu.VMEM(*lattice), pltpu.SemaphoreType.DMA((CHUNKS,))]
        else:
            outs, specs = [lattice, plane, square, lanes], None
            scratch = [pltpu.VMEM(*plane), pltpu.VMEM(*wide)]
        streamed = call(
            functools.partial(stream_kernel, final, step > 0), "stream",
            inputs, [VM] * len(inputs), outs, out_specs=specs, scratch=scratch, us=4,
        )
        rxu, rxd, streamed = lax.optimization_barrier((rxu, rxd, streamed))
        ryu, ryd = exchange(
            "gy",
            jnp.concatenate([yu, rxd[32:48], rxu[32:48]], axis=0),
            jnp.concatenate([yd, rxd[0:16], rxu[0:16]], axis=0),
        )
        received = (rxu, rxd, ryu, ryd)
        if step == 0:
            rc, halves = call(
                prepare_kernel, "prepare", (rate, blocks), [VM, VM], [plane, ((PB, 4, BLK, 256), BF16)], us=1
            )
        inputs = (live_count, prof, radial, rc) + (() if step == 0 else (base, flow, conc))
        if final:
            outs, specs = [plane, ((2, SLOTS, NR), F32)], [VM, HBM]
            scratch = [pltpu.VMEM(*plane), pltpu.SemaphoreType.DMA((4,))]
        else:
            outs, specs, scratch = [plane, shells, plane], None, []
        mixed = call(
            functools.partial(mix_kernel, step == 0, final), "mix",
            inputs, [SM] + [VM] * (len(inputs) - 1), outs, out_specs=specs, scratch=scratch, us=1,
        )
        if final:
            return call(
                last_kernel, "last",
                (live_count, cols, prof, mixed[0], ex, tt, halves, *received, *streamed[1:],
                 mixed[1], streamed[0].reshape(7, CX, 32, 128)),
                [SM] * 2 + [VM] * 11 + [HBM] * 2,
                [((2, SLOTS, NR), F32), ((7, CX, 32, 128), F32)],
                out_specs=[HBM, HBM],
                scratch=[ext_s, pltpu.VMEM(*shells), pltpu.VMEM(*plane)] + [pltpu.VMEM((32, 128), F32)] * 2
                + [pltpu.VMEM((CX, 8, 128), F32)] * 2 + [pltpu.SemaphoreType.DMA((8,))],
                aliases={13: 0, 14: 1},
            )
        base, ttb, conc = mixed
        pops, theta, edge, there = streamed
        flow, tt, theta, faces, ex, vt, xu, xd, yu, yd = call(
            middle_kernel, "middle",
            (live_count, cols, ex, tt, ttb, halves, *received, theta, there, edge, cell, coef, otf, slt),
            [SM] * 2 + [VM] * 15,
            [shells, shells, plane, square, lanes, wide] + sends,
            scratch=[ext_s],
        )


def solution(mesh):
    return jax.shard_map(
        on_device,
        mesh=mesh,
        in_specs=(
            P(None, ("gx", "gy"), None),
            P(),
            P(("gx", "gy")),
            P(("gx", "gy")),
            P(("gx", "gy")),
            P(("gx", "gy"), None),
            P(("gx", "gy")),
            P(("gx", "gy"), None),
            P(("gx", "gy"), None, None, None),
            P(None, "gx", "gy", None),
        ),
        out_specs=(P(None, ("gx", "gy"), None), P(None, "gx", "gy", None)),
        check_vma=False,
    )
```

```python
import functools

import jax
import jax.numpy as jnp
from jax import lax
from jax.experimental import pallas as pl
from jax.experimental.pallas import tpu as pltpu
from jax.sharding import PartitionSpec as P

NR = 128
BLK = 128
SHELL = 16
STEPS = 3
PB = 8
SLOTS = PB * BLK
CX = 32
CELLS = 1024
CHUNKS = 4
CHUNK = CELLS // CHUNKS
F32 = jnp.float32
BF16 = jnp.bfloat16

OFFSETS = ((-1, -1), (-1, 0), (-1, 1), (0, -1), (0, 1), (1, -1), (1, 0), (1, 1))
NT = (((1,), (1,)), ((), ()))
NN = (((1,), (0,)), ((), ()))
VM = pl.BlockSpec(memory_space=pltpu.VMEM)
SM = pl.BlockSpec(memory_space=pltpu.SMEM)
HBM = pl.BlockSpec(memory_space=pltpu.HBM)

FACES = (slice(992, 1024), slice(0, 32), pl.ds(31, 32, stride=32), pl.ds(0, 32, stride=32))


def dot(a, b, dims=NN):
    return lax.dot_general(a, b, dims, preferred_element_type=F32)


def split2(x):
    hi = x.astype(BF16)
    return hi, (x - hi.astype(F32)).astype(BF16)


def split3(x):
    hi = x.astype(BF16)
    rest = x - hi.astype(F32)
    mid = rest.astype(BF16)
    return hi, mid, (rest - mid.astype(F32)).astype(BF16)


def flag(cond):
    return jnp.where(cond, 1.0, 0.0).astype(F32)


def neighbour(n):
    a, b = OFFSETS[n]
    x, y = lax.axis_index("gx") - a, lax.axis_index("gy") - b
    return flag((x >= 0) & (x < lax.axis_size("gx")) & (y >= 0) & (y < lax.axis_size("gy")))


def halves_of(g):
    return g[:, 0:128] + g[:, 128:256]


def pair(ref, j):
    return jnp.concatenate([ref[2 * j : 2 * j + 1, :], ref[2 * j + 1 : 2 * j + 2, :]], axis=1)


def store_pair(ref, j, row):
    ref[2 * j : 2 * j + 1, :] = row[:, 0:128]
    ref[2 * j + 1 : 2 * j + 2, :] = row[:, 128:256]


def lane_mask(cell, j):
    return lax.broadcasted_iota(jnp.int32, (128, 256), 0) == (pair(cell, j) & 127)


def pick(mask, g):
    return jnp.sum(jnp.where(mask, g, 0.0), axis=0, keepdims=True)


def send_ghosts(tt, lists, xu, xd, yu, yd):
    places = ((xd, 0), (xd, 16), (xd, 32), (yd, 0), (yu, 0), (xu, 0), (xu, 16), (xu, 32))
    for n in range(8):
        listed = jnp.broadcast_to(lists[n : n + 1, :], (8, BLK))
        lane, block = listed & 127, listed >> 7
        ref, start = places[n]
        for h in (0, 8):
            total = None
            for b in range(PB):
                shell = tt[h : h + 8, b * BLK : (b + 1) * BLK]
                g = jnp.take_along_axis(shell, lane, axis=1, mode="promise_in_bounds")
                total = g if b == 0 else jnp.where(block == b, g, total)
            ref[start + h : start + h + 8, :] = total


def send_faces(there, theta, edge, tt, cell, coef, blocks, otf, ex, vt, xu, xd, yu, yd):
    for j in range(4):
        at = slice(j * 256, (j + 1) * 256)
        alive = jnp.concatenate(
            [jnp.full((1, 128), flag(2 * j + h < blocks), F32) for h in range(2)], axis=1
        )
        e = pair(coef, j) * (there[j] - tt[15:16, at]) * alive
        store_pair(ex, j, e)
        hi, lo = split2(jnp.where(lane_mask(cell, j), e, 0.0))
        vt[0:128, at] = hi
        vt[128:256, at] = lo
    source = halves_of(dot(otf[0:128, :], vt[...], NT))
    outs = ((xu, 48), (xd, 48), (yu, 16), (yd, 16))
    for f in range(4):
        ref, start = outs[f]
        rows = slice(f * 32, (f + 1) * 32)
        s = 1.25 * theta[FACES[f], :] - 0.5 * source[rows, :]
        ref[start : start + 32, :] = 0.125 * s - 0.25 * edge[rows, :]


def first_kernel(
    live, cell_in, coef_in, lists_in, prof_in, pops_in,
    cell, coef, lists, prof, pops, ot, otf, tt, theta, ex, vt, xu, xd, yu, yd,
    gathered, edge, sems,
):
    blocks = live[0] // BLK
    copies = [
        pltpu.make_async_copy(cell_in, cell, sems.at[0]),
        pltpu.make_async_copy(lists_in, lists, sems.at[1]),
        pltpu.make_async_copy(prof_in.at[0], prof.at[0], sems.at[2]),
    ]
    for c in range(CHUNKS):
        rows = pl.ds(c * CHUNK, CHUNK)
        copies.append(pltpu.make_async_copy(pops_in.at[:, rows, :], pops.at[:, rows, :], sems.at[3 + c]))
    copies.append(pltpu.make_async_copy(coef_in, coef, sems.at[3 + CHUNKS]))
    copies.append(pltpu.make_async_copy(prof_in.at[1], prof.at[1], sems.at[4 + CHUNKS]))
    for c in copies:
        c.start()
    sub = lax.broadcasted_iota(jnp.int32, (CELLS, BLK), 0)
    f = lax.broadcasted_iota(jnp.int32, (128, BLK), 0)
    f_row = jnp.where(f < 32, f + 992, jnp.where(f < 64, f - 32, jnp.where(f < 96, f * 32 - 2017, f * 32 - 3072)))
    copies[0].wait()
    for b in range(PB):
        at = slice(b * BLK, (b + 1) * BLK)
        row = cell[b : b + 1, :] >> 7
        ot[:, at] = jnp.where(sub == row, 1.0, 0.0).astype(BF16)
        face = jnp.where(f_row == row, 1.0, 0.0).astype(BF16)
        otf[0:128, at] = face
        otf[128:256, at] = face
    copies[1].wait()
    copies[2].wait()
    for b in range(PB):
        at = slice(b * BLK, (b + 1) * BLK)
        tt[:, at] = prof[0, at, :].T[NR - SHELL :, :]
    send_ghosts(tt, lists, xu, xd, yu, yd)
    for c in range(CHUNKS):
        copies[3 + c].wait()
        parts = []
        for h in range(CHUNK // 128):
            at = slice(c * CHUNK + h * 128, c * CHUNK + (h + 1) * 128)
            total = pops[0, at, :]
            for i in range(1, 7):
                total = total + pops[i, at, :]
            theta[at, :] = total
            parts.append(jnp.concatenate(split2(total.T), axis=0))
        rows = jnp.concatenate(parts, axis=1)
        for j in range(4):
            at = slice(j * 256, (j + 1) * 256)
            g = dot(rows, ot[c * CHUNK : (c + 1) * CHUNK, at])
            gathered[:, at] = g if c == 0 else gathered[:, at] + g
    for i in range(4):
        edge[i * 32 : (i + 1) * 32, :] = pops[i + 1, FACES[i], :]
    copies[3 + CHUNKS].wait()
    there = []
    for j in range(4):
        at = slice(j * 256, (j + 1) * 256)
        there.append(pick(lane_mask(cell, j), gathered[0:128, at] + gathered[128:256, at]))
    send_faces(there, theta, edge, tt, cell, coef, blocks, otf, ex, vt, xu, xd, yu, yd)
    copies[4 + CHUNKS].wait()


def stream_kernel(last, has_faces, *refs):
    if has_faces:
        faces, refs = refs[0], refs[1:]
    if last:
        pops, theta, vt, ot, out, strip3, strip4, source, new, sems = refs
    else:
        pops, theta, vt, ot, new, theta_new, edge, source = refs
    for j in range(4):
        at = slice(j * 256, (j + 1) * 256)
        source[at, :] = 1.25 * theta[at, :] - 0.5 * halves_of(dot(ot[at, :], vt[...], NT))
    y = lax.broadcasted_iota(jnp.int32, (32, 128), 0)
    z = lax.broadcasted_iota(jnp.int32, (32, 128), 1)

    def row(x, _):
        at = pl.ds(pl.multiple_of(x * 32, 32), 32)
        before = pl.ds(pl.multiple_of(jnp.maximum(x - 1, 0) * 32, 32), 32)
        after = pl.ds(pl.multiple_of(jnp.minimum(x + 1, CX - 1) * 32, 32), 32)
        s = 0.125 * source[at, :]
        n0 = 2.0 * s - 0.25 * pops[0, at, :]
        new[0, at, :] = n0
        n1 = flag(x > 0) * (0.125 * source[before, :] - 0.25 * pops[1, before, :])
        new[1, at, :] = n1
        n2 = flag(x < CX - 1) * (0.125 * source[after, :] - 0.25 * pops[2, after, :])
        new[2, at, :] = n2
        n3 = jnp.where(y == 0, 0.0, pltpu.roll(s - 0.25 * pops[3, at, :], 1, 0))
        new[3, at, :] = n3
        n4 = jnp.where(y == 31, 0.0, pltpu.roll(s - 0.25 * pops[4, at, :], 31, 0))
        new[4, at, :] = n4
        n5 = jnp.where(z == 0, 0.0, pltpu.roll(s - 0.25 * pops[5, at, :], 1, 1))
        new[5, at, :] = n5
        n6 = jnp.where(z == 127, 0.0, pltpu.roll(s - 0.25 * pops[6, at, :], 127, 1))
        new[6, at, :] = n6
        if not last:
            theta_new[at, :] = ((n0 + n1) + (n2 + n3)) + ((n4 + n5) + n6)
        return 0

    def carry_faces(c):
        parts = (
            (0, 1, slice(32, 64), faces[32:64, :]),
            (CHUNKS - 1, 2, slice(960, 992), faces[0:32, :]),
            (c, 3, pl.ds(c * CHUNK + 1, 8, stride=32), faces[96 + c * 8 : 104 + c * 8, :]),
            (c, 4, pl.ds(c * CHUNK + 30, 8, stride=32), faces[64 + c * 8 : 72 + c * 8, :]),
        )
        for chunk, i, at, face in parts:
            if chunk == c:
                new[i, at, :] = new[i, at, :] - 0.25 * face
                if not last:
                    theta_new[at, :] = theta_new[at, :] - 0.25 * face

    copies = []
    for c in range(CHUNKS):
        lax.fori_loop(c * 8, (c + 1) * 8, row, 0, unroll=2)
        if has_faces:
            carry_faces(c)
        if last:
            at = pl.ds(c * CHUNK, CHUNK)
            copies.append(pltpu.make_async_copy(new.at[:, at, :], out.at[:, at, :], sems.at[c]))
            copies[-1].start()
            for x in range(c * 8, (c + 1) * 8):
                strip3[x] = new[3, x * 32 : x * 32 + 8, :]
                strip4[x] = new[4, x * 32 + 24 : x * 32 + 32, :]
    if last:
        for copy in copies:
            copy.wait()
        return
    for i in range(4):
        edge[i * 32 : (i + 1) * 32, :] = new[i + 1, FACES[i], :]


def gather_kernel(theta, ot, cell, there, rows):
    for b in range(PB):
        at = slice(b * BLK, (b + 1) * BLK)
        hi, lo = split2(theta[at, :].T)
        rows[0:128, at] = hi
        rows[128:256, at] = lo
    for j in range(4):
        g = dot(rows[...], ot[:, j * 256 : (j + 1) * 256])
        store_pair(there, j, pick(lane_mask(cell, j), g[0:128, :] + g[128:256, :]))


def prepare_kernel(rate, blocks, rc, halves):
    for b in range(PB):
        rc[b * BLK : (b + 1) * BLK, :] = jnp.broadcast_to(rate[b : b + 1, :], (BLK, NR)).T
        for k in range(4):
            hi, lo = split2(blocks[b, k].T)
            halves[b, k * 256 : k * 256 + 128, :] = hi
            halves[b, k * 256 + 128 : k * 256 + 256, :] = lo


def temp_now(b, at, blocks, prof, base, flow):
    added = jnp.concatenate([jnp.zeros((NR - SHELL, BLK), F32), flow[:, at]], axis=0).T
    alive = flag(b < blocks)
    return alive * (base[at, :] + added) + (1.0 - alive) * prof[0, at, :]


def mix_kernel(first, last, *refs):
    if first:
        live, prof, radial, rc, *refs = refs
    else:
        live, prof, radial, rc, base_in, flow, conc_in, *refs = refs
    if last:
        base, out, conc_new, sems = refs
    else:
        base, ttb, conc_new = refs
    blocks = live[0] // BLK
    wide = []
    for c in range(2):
        hi, lo = split2(radial[c])
        top = jnp.concatenate([hi, lo], axis=1)
        wide.append(jnp.concatenate([top, jnp.concatenate([hi, jnp.zeros_like(hi)], axis=1)], axis=0))
    copies = []
    for b in range(PB):
        at = slice(b * BLK, (b + 1) * BLK)
        conc = prof[1, at, :] if first else conc_in[at, :]
        temp = prof[0, at, :] if first else temp_now(b, at, blocks, prof, base_in, flow)
        alive = flag(b < blocks)
        rate = rc[at, :] * conc * jnp.exp(0.5 * jnp.tanh(temp - 1.0))
        value = halves_of(dot(jnp.concatenate(split2(temp), axis=1), wide[0])) + rate
        base[at, :] = value
        if not last:
            ttb[:, at] = value.T[NR - SHELL :, :]
        value = halves_of(dot(jnp.concatenate(split2(conc), axis=1), wide[1])) - rate
        conc_new[at, :] = alive * value + (1.0 - alive) * conc
        if last and b % 2 == 1:
            two = pl.ds((b - 1) * BLK, 2 * BLK)
            copies.append(pltpu.make_async_copy(conc_new.at[two, :], out.at[1, two, :], sems.at[b // 2]))
            copies[-1].start()
    for copy in copies:
        copy.wait()


def extend(blocks, tt, rxu, rxd, ryu, ryd, extended):
    for b in range(PB):
        alive = flag(b < blocks)
        hi, lo = split2(tt[:, b * BLK : (b + 1) * BLK] * alive)
        extended[b, 0:16, :] = hi
        extended[b, 16:32, :] = lo
        extended[b, 32:48, :] = jnp.full((16, 128), alive, F32).astype(BF16)
    places = ((ryd, 48), (rxd, 16), (ryu, 48), (ryd, 0), (ryu, 0), (ryd, 64), (rxu, 16), (ryu, 64))
    for n in range(8):
        ref, start = places[n]
        there = neighbour(n)
        hi, lo = split2(ref[start : start + 16, :] * there)
        extended[8 + n, 0:16, :] = hi
        extended[8 + n, 16:32, :] = lo
        extended[8 + n, 32:48, :] = jnp.full((16, 128), there, F32).astype(BF16)


def contact_part(cols, ex, tt, halves, extended, store):
    row = lax.broadcasted_iota(jnp.int32, (16, 128), 0)
    for b in range(PB):
        at = slice(b * BLK, (b + 1) * BLK)
        picked = [extended[cols[k // 2, b]] for k in range(8)]
        total = dot(jnp.concatenate(picked, axis=1), halves[b])
        flow = total[0:16, :] + total[16:32, :] - total[32:33, :] * tt[:, at]
        store(b, at, jnp.where(row == 15, flow + ex[b : b + 1, :], flow))


def middle_kernel(
    live, cols_in, ex_in, tt_in, ttb, halves, rxu, rxd, ryu, ryd, theta_in, there_in, edge, cell, coef, otf, lists,
    flow, tt, theta, faces, ex, vt, xu, xd, yu, yd, extended, cols, sem,
):
    fetch = pltpu.make_async_copy(cols_in, cols, sem)
    fetch.start()
    blocks = live[0] // BLK
    extend(blocks, tt_in, rxu, rxd, ryu, ryd, extended)
    theta[...] = theta_in[...]
    came = ((rxd, 48, 1), (rxu, 48, 6), (ryd, 16, 3), (ryu, 16, 4))
    for f in range(4):
        ref, start, n = came[f]
        face = ref[start : start + 32, :] * neighbour(n)
        faces[f * 32 : (f + 1) * 32, :] = face
        theta[FACES[f], :] = theta[FACES[f], :] + face
    rows = jnp.concatenate(split2(faces[...].T), axis=1)
    there = []
    for j in range(4):
        more = pick(lane_mask(cell, j), dot(rows, otf[:, j * 256 : (j + 1) * 256]))
        there.append(pair(there_in, j) + more)
    fetch.wait()

    def store(b, at, value):
        flow[:, at] = value
        alive = flag(b < blocks)
        tt[:, at] = alive * (ttb[:, at] + value) + (1.0 - alive) * tt_in[:, at]

    contact_part(cols, ex_in, tt_in, halves, extended, store)
    send_ghosts(tt, lists, xu, xd, yu, yd)
    send_faces(there, theta, edge, tt, cell, coef, blocks, otf, ex, vt, xu, xd, yu, yd)


def last_kernel(
    live, cols_in, prof, base, ex, tt, halves, rxu, rxd, ryu, ryd, strip3, strip4, prof_in, pops_in,
    profiles, pops, extended, flow, temp, face1, face2, patch3, patch4, cols, sems,
):
    fetch = pltpu.make_async_copy(cols_in, cols, sems.at[8])
    fetch.start()
    blocks = live[0] // BLK
    face1[...] = rxu[48:80, :] * neighbour(6)
    face2[...] = rxd[48:80, :] * neighbour(1)
    y = lax.broadcasted_iota(jnp.int32, (8, 128), 0)
    for x in range(CX):
        patch3[x] = jnp.where(y == 0, ryu[16 + x : 17 + x, :] * neighbour(4), strip3[x])
        patch4[x] = jnp.where(y == 7, ryd[16 + x : 17 + x, :] * neighbour(3), strip4[x])
    copies = [
        pltpu.make_async_copy(face1, pops.at[1, 0], sems.at[0]),
        pltpu.make_async_copy(face2, pops.at[2, CX - 1], sems.at[1]),
        pltpu.make_async_copy(patch3, pops.at[3, :, 0:8, :], sems.at[2]),
        pltpu.make_async_copy(patch4, pops.at[4, :, 24:32, :], sems.at[3]),
    ]
    for c in copies:
        c.start()

    def store(b, at, value):
        flow[:, at] = value
        temp[at, :] = temp_now(b, at, blocks, prof, base, flow)
        if b % 2 == 1:
            two = pl.ds((b - 1) * BLK, 2 * BLK)
            copies.append(pltpu.make_async_copy(temp.at[two, :], profiles.at[0, two, :], sems.at[4 + b // 2]))
            copies[-1].start()

    extend(blocks, tt, rxu, rxd, ryu, ryd, extended)
    fetch.wait()
    contact_part(cols, ex, tt, halves, extended, store)
    for c in copies:
        c.wait()


def call(kernel, name, ins, in_specs, outs, out_specs=None, scratch=(), us=2, aliases=None, mib=8):
    shapes = [jax.ShapeDtypeStruct(s, d) for s, d in outs]
    return pl.pallas_call(
        kernel,
        name=name,
        out_shape=shapes,
        in_specs=in_specs,
        out_specs=[VM] * len(outs) if out_specs is None else out_specs,
        scratch_shapes=list(scratch),
        compiler_params=pltpu.CompilerParams(vmem_limit_bytes=mib * 1024 * 1024),
        input_output_aliases=aliases or {},
        cost_estimate=pl.CostEstimate(flops=us * 10**8, bytes_accessed=us * 3 * 10**6, transcendentals=0),
    )(*ins)


def exchange(axis, to_up, to_down):
    n = lax.axis_size(axis)
    up = [(i, (i + 1) % n) for i in range(n)]
    down = [(j, i) for i, j in up]
    return lax.ppermute(to_up, axis, up), lax.ppermute(to_down, axis, down)


def on_device(
    profiles, radial, rate_const, transfer_coef, live_count, send_lists, cell_index, contact_cols, contact_blocks, populations
):
    blocks = contact_blocks.reshape(PB, 4, BLK, BLK)
    rate = rate_const.reshape(PB, BLK)
    cols = contact_cols.T
    plane, lanes, shells, square = ((SLOTS, 128), F32), ((PB, BLK), F32), ((SHELL, SLOTS), F32), ((128, 128), F32)
    lattice = ((7, CELLS, 128), F32)
    wide = ((256, 1024), BF16)
    sends = [((80, 128), F32)] * 2 + [((48, 128), F32)] * 2
    cols_s = pltpu.SMEM((4, PB), jnp.int32)
    ext_s = pltpu.VMEM((16, 48, 128), BF16)

    stay = [
        pltpu.with_memory_space_constraint(a, pltpu.HBM)
        for a in (
            cell_index.reshape(PB, BLK),
            transfer_coef.reshape(PB, BLK),
            send_lists,
            profiles,
            populations.reshape(7, CELLS, 128),
        )
    ]
    cell, coef, lists, prof, pops, ot, otf, tt, theta, ex, vt, xu, xd, yu, yd = call(
        first_kernel, "first", (live_count, *stay),
        [SM] + [HBM] * 5,
        [((PB, BLK), jnp.int32), lanes, ((PB, BLK), jnp.int32), ((2, SLOTS, NR), F32), lattice, ((CELLS, SLOTS), BF16), wide,
         shells, plane, lanes, wide] + sends,
        scratch=[pltpu.VMEM((256, 1024), F32), pltpu.VMEM((128, 128), F32),
                 pltpu.SemaphoreType.DMA((5 + CHUNKS,))],
        us=6,
    )
    faces = base = flow = conc = there = edge = None
    for step in range(STEPS):
        final = step == STEPS - 1
        rxu, rxd = exchange("gx", xu, xd)
        inputs = (() if step == 0 else (faces,)) + (pops, theta, vt, ot)
        if final:
            outs, specs = [lattice] + [((CX, 8, 128), F32)] * 2, [HBM, VM, VM]
            scratch = [pltpu.VMEM(*plane), pltpu.VMEM(*lattice), pltpu.SemaphoreType.DMA((CHUNKS,))]
        else:
            outs, specs = [lattice, plane, square], None
            scratch = [pltpu.VMEM(*plane)]
        streamed = call(
            functools.partial(stream_kernel, final, step > 0), "stream",
            inputs, [VM] * len(inputs), outs, out_specs=specs, scratch=scratch, us=3,
        )
        if step == 0:
            rc, halves = call(
                prepare_kernel, "prepare", (rate, blocks), [VM, VM], [plane, ((PB, 1024, BLK), BF16)], us=1
            )
        inputs = (live_count, prof, radial, rc) + (() if step == 0 else (base, flow, conc))
        if final:
            outs, specs = [plane, ((2, SLOTS, NR), F32)], [VM, HBM]
            scratch = [pltpu.VMEM(*plane), pltpu.SemaphoreType.DMA((4,))]
        else:
            outs, specs, scratch = [plane, shells, plane], None, []
        mixed = call(
            functools.partial(mix_kernel, step == 0, final), "mix",
            inputs, [SM] + [VM] * (len(inputs) - 1), outs, out_specs=specs, scratch=scratch, us=1,
        )
        if final:
            rxu, rxd, mixed = lax.optimization_barrier((rxu, rxd, mixed))
        else:
            rxu, rxd, streamed = lax.optimization_barrier((rxu, rxd, streamed))
        ryu, ryd = exchange(
            "gy",
            jnp.concatenate([yu, rxd[32:48], rxu[32:48]], axis=0),
            jnp.concatenate([yd, rxd[0:16], rxu[0:16]], axis=0),
        )
        received = (rxu, rxd, ryu, ryd)
        if final:
            return call(
                last_kernel, "last",
                (live_count, cols, prof, mixed[0], ex, tt, halves, *received, *streamed[1:],
                 mixed[1], streamed[0].reshape(7, CX, 32, 128)),
                [SM] + [VM] * 12 + [HBM] * 2,
                [((2, SLOTS, NR), F32), ((7, CX, 32, 128), F32)],
                out_specs=[HBM, HBM],
                scratch=[ext_s, pltpu.VMEM(*shells), pltpu.VMEM(*plane)] + [pltpu.VMEM((32, 128), F32)] * 2
                + [pltpu.VMEM((CX, 8, 128), F32)] * 2 + [cols_s, pltpu.SemaphoreType.DMA((9,))],
                aliases={13: 0, 14: 1},
            )
        base, ttb, conc = mixed
        pops, theta, edge = streamed
        (there,) = call(
            gather_kernel, "gather", (theta, ot, cell), [VM] * 3, [lanes], scratch=[pltpu.VMEM(*wide)], us=1
        )
        flow, tt, theta, faces, ex, vt, xu, xd, yu, yd = call(
            middle_kernel, "middle",
            (live_count, cols, ex, tt, ttb, halves, *received, theta, there, edge, cell, coef, otf, lists),
            [SM] + [VM] * 16,
            [shells, shells, plane, square, lanes, wide] + sends,
            scratch=[ext_s, cols_s, pltpu.SemaphoreType.DMA],
        )


def solution(mesh):
    return jax.shard_map(
        on_device,
        mesh=mesh,
        in_specs=(
            P(None, ("gx", "gy"), None),
            P(),
            P(("gx", "gy")),
            P(("gx", "gy")),
            P(("gx", "gy")),
            P(("gx", "gy"), None),
            P(("gx", "gy")),
            P(("gx", "gy"), None),
            P(("gx", "gy"), None, None, None),
            P(None, "gx", "gy", None),
        ),
        out_specs=(P(None, ("gx", "gy"), None), P(None, "gx", "gy", None)),
        check_vma=False,
    )
```

```python
import functools

import jax
import jax.numpy as jnp
from jax import lax
from jax.experimental import pallas as pl
from jax.experimental.pallas import tpu as pltpu
from jax.sharding import PartitionSpec as P

NR = 128
BLK = 128
SHELL = 16
STEPS = 3
PB = 8
SLOTS = PB * BLK
CX = 32
CELLS = 1024
CHUNKS = 4
CHUNK = CELLS // CHUNKS
F32 = jnp.float32
BF16 = jnp.bfloat16

OFFSETS = ((-1, -1), (-1, 0), (-1, 1), (0, -1), (0, 1), (1, -1), (1, 0), (1, 1))
NT = (((1,), (1,)), ((), ()))
NN = (((1,), (0,)), ((), ()))
VM = pl.BlockSpec(memory_space=pltpu.VMEM)
SM = pl.BlockSpec(memory_space=pltpu.SMEM)
HBM = pl.BlockSpec(memory_space=pltpu.HBM)

FACES = (slice(992, 1024), slice(0, 32), pl.ds(31, 32, stride=32), pl.ds(0, 32, stride=32))


def dot(a, b, dims=NN):
    return lax.dot_general(a, b, dims, preferred_element_type=F32)


def split2(x):
    hi = x.astype(BF16)
    return hi, (x - hi.astype(F32)).astype(BF16)


def split3(x):
    hi = x.astype(BF16)
    rest = x - hi.astype(F32)
    mid = rest.astype(BF16)
    return hi, mid, (rest - mid.astype(F32)).astype(BF16)


def flag(cond):
    return jnp.where(cond, 1.0, 0.0).astype(F32)


def neighbour(n):
    a, b = OFFSETS[n]
    x, y = lax.axis_index("gx") - a, lax.axis_index("gy") - b
    return flag((x >= 0) & (x < lax.axis_size("gx")) & (y >= 0) & (y < lax.axis_size("gy")))


def halves_of(g):
    return g[:, 0:128] + g[:, 128:256]


def pair(ref, j):
    return jnp.concatenate([ref[2 * j : 2 * j + 1, :], ref[2 * j + 1 : 2 * j + 2, :]], axis=1)


def store_pair(ref, j, row):
    ref[2 * j : 2 * j + 1, :] = row[:, 0:128]
    ref[2 * j + 1 : 2 * j + 2, :] = row[:, 128:256]


def lane_mask(cell, j):
    return lax.broadcasted_iota(jnp.int32, (128, 256), 0) == (pair(cell, j) & 127)


def pick(mask, g):
    return jnp.sum(jnp.where(mask, g, 0.0), axis=0, keepdims=True)


def send_ghosts(tt, lists, xu, xd, yu, yd):
    places = ((xd, 0), (xd, 16), (xd, 32), (yd, 0), (yu, 0), (xu, 0), (xu, 16), (xu, 32))
    for n in range(8):
        listed = jnp.broadcast_to(lists[n : n + 1, :], (8, BLK))
        lane, block = listed & 127, listed >> 7
        ref, start = places[n]
        for h in (0, 8):
            total = None
            for b in range(PB):
                shell = tt[h : h + 8, b * BLK : (b + 1) * BLK]
                g = jnp.take_along_axis(shell, lane, axis=1, mode="promise_in_bounds")
                total = g if b == 0 else jnp.where(block == b, g, total)
            ref[start + h : start + h + 8, :] = total


def send_faces(there, theta, edge, tt, cell, coef, blocks, otf, ex, vt, xu, xd, yu, yd):
    for j in range(4):
        at = slice(j * 256, (j + 1) * 256)
        alive = jnp.concatenate(
            [jnp.full((1, 128), flag(2 * j + h < blocks), F32) for h in range(2)], axis=1
        )
        e = pair(coef, j) * (there[j] - tt[15:16, at]) * alive
        store_pair(ex, j, e)
        hi, lo = split2(jnp.where(lane_mask(cell, j), e, 0.0))
        vt[0:128, at] = hi
        vt[128:256, at] = lo
    source = halves_of(dot(otf[0:128, :], vt[...], NT))
    outs = ((xu, 48), (xd, 48), (yu, 16), (yd, 16))
    for f in range(4):
        ref, start = outs[f]
        rows = slice(f * 32, (f + 1) * 32)
        s = 1.25 * theta[FACES[f], :] - 0.5 * source[rows, :]
        ref[start : start + 32, :] = 0.125 * s - 0.25 * edge[rows, :]


def first_kernel(
    live, cell_in, coef_in, lists_in, prof_in, pops_in,
    cell, coef, lists, prof, pops, ot, otf, tt, theta, ex, vt, xu, xd, yu, yd,
    gathered, rows, edge, sems,
):
    blocks = live[0] // BLK
    copies = [
        pltpu.make_async_copy(cell_in, cell, sems.at[0]),
        pltpu.make_async_copy(lists_in, lists, sems.at[1]),
        pltpu.make_async_copy(prof_in.at[0], prof.at[0], sems.at[2]),
    ]
    for c in range(CHUNKS):
        part = pl.ds(c * CHUNK, CHUNK)
        copies.append(pltpu.make_async_copy(pops_in.at[:, part, :], pops.at[:, part, :], sems.at[3 + c]))
    copies.append(pltpu.make_async_copy(coef_in, coef, sems.at[3 + CHUNKS]))
    copies.append(pltpu.make_async_copy(prof_in.at[1], prof.at[1], sems.at[4 + CHUNKS]))
    for c in copies:
        c.start()
    sub = lax.broadcasted_iota(jnp.int32, (CELLS, BLK), 0)
    f = lax.broadcasted_iota(jnp.int32, (128, BLK), 0)
    f_row = jnp.where(f < 32, f + 992, jnp.where(f < 64, f - 32, jnp.where(f < 96, f * 32 - 2017, f * 32 - 3072)))
    copies[0].wait()
    for b in range(PB):
        at = slice(b * BLK, (b + 1) * BLK)
        row = cell[b : b + 1, :] >> 7
        ot[:, at] = jnp.where(sub == row, 1.0, 0.0).astype(BF16)
        face = jnp.where(f_row == row, 1.0, 0.0).astype(BF16)
        otf[0:128, at] = face
        otf[128:256, at] = face
    copies[1].wait()
    copies[2].wait()
    for b in range(PB):
        at = slice(b * BLK, (b + 1) * BLK)
        tt[:, at] = prof[0, at, :].T[NR - SHELL :, :]
    send_ghosts(tt, lists, xu, xd, yu, yd)
    for c in range(CHUNKS):
        copies[3 + c].wait()
        for h in range(CHUNK // 128):
            at = slice(c * CHUNK + h * 128, c * CHUNK + (h + 1) * 128)
            total = pops[0, at, :]
            for i in range(1, 7):
                total = total + pops[i, at, :]
            theta[at, :] = total
            hi, lo = split2(total.T)
            rows[0:128, at] = hi
            rows[128:256, at] = lo
        if c == CHUNKS - 2:
            for j in range(4):
                at = slice(j * 256, (j + 1) * 256)
                gathered[:, at] = dot(rows[:, 0 : (c + 1) * CHUNK], ot[0 : (c + 1) * CHUNK, at])
    for i in range(4):
        edge[i * 32 : (i + 1) * 32, :] = pops[i + 1, FACES[i], :]
    copies[3 + CHUNKS].wait()
    there = []
    for j in range(4):
        at = slice(j * 256, (j + 1) * 256)
        g = gathered[:, at] + dot(rows[:, CELLS - CHUNK :], ot[CELLS - CHUNK :, at])
        there.append(pick(lane_mask(cell, j), g[0:128, :] + g[128:256, :]))
    send_faces(there, theta, edge, tt, cell, coef, blocks, otf, ex, vt, xu, xd, yu, yd)
    copies[4 + CHUNKS].wait()


def stream_kernel(last, has_faces, *refs):
    if has_faces:
        faces, refs = refs[0], refs[1:]
    if last:
        pops, theta, vt, ot, new, source = refs
    else:
        pops, theta, vt, ot, new, theta_new, edge, source = refs
    for j in range(4):
        at = slice(j * 256, (j + 1) * 256)
        source[at, :] = 1.25 * theta[at, :] - 0.5 * halves_of(dot(ot[at, :], vt[...], NT))
    y = lax.broadcasted_iota(jnp.int32, (32, 128), 0)
    z = lax.broadcasted_iota(jnp.int32, (32, 128), 1)

    def row(x, _):
        at = pl.ds(pl.multiple_of(x * 32, 32), 32)
        before = pl.ds(pl.multiple_of(jnp.maximum(x - 1, 0) * 32, 32), 32)
        after = pl.ds(pl.multiple_of(jnp.minimum(x + 1, CX - 1) * 32, 32), 32)
        s = 0.125 * source[at, :]
        n0 = 2.0 * s - 0.25 * pops[0, at, :]
        new[0, at, :] = n0
        n1 = flag(x > 0) * (0.125 * source[before, :] - 0.25 * pops[1, before, :])
        new[1, at, :] = n1
        n2 = flag(x < CX - 1) * (0.125 * source[after, :] - 0.25 * pops[2, after, :])
        new[2, at, :] = n2
        n3 = jnp.where(y == 0, 0.0, pltpu.roll(s - 0.25 * pops[3, at, :], 1, 0))
        new[3, at, :] = n3
        n4 = jnp.where(y == 31, 0.0, pltpu.roll(s - 0.25 * pops[4, at, :], 31, 0))
        new[4, at, :] = n4
        n5 = jnp.where(z == 0, 0.0, pltpu.roll(s - 0.25 * pops[5, at, :], 1, 1))
        new[5, at, :] = n5
        n6 = jnp.where(z == 127, 0.0, pltpu.roll(s - 0.25 * pops[6, at, :], 127, 1))
        new[6, at, :] = n6
        if not last:
            theta_new[at, :] = ((n0 + n1) + (n2 + n3)) + ((n4 + n5) + n6)
        return 0

    def carry_faces(c):
        parts = (
            (0, 1, slice(32, 64), faces[32:64, :]),
            (CHUNKS - 1, 2, slice(960, 992), faces[0:32, :]),
            (c, 3, pl.ds(c * CHUNK + 1, 8, stride=32), faces[96 + c * 8 : 104 + c * 8, :]),
            (c, 4, pl.ds(c * CHUNK + 30, 8, stride=32), faces[64 + c * 8 : 72 + c * 8, :]),
        )
        for chunk, i, at, face in parts:
            if chunk == c:
                new[i, at, :] = new[i, at, :] - 0.25 * face
                if not last:
                    theta_new[at, :] = theta_new[at, :] - 0.25 * face

    for c in range(CHUNKS):
        lax.fori_loop(c * 8, (c + 1) * 8, row, 0, unroll=2)
        if has_faces:
            carry_faces(c)
    if last:
        return
    for i in range(4):
        edge[i * 32 : (i + 1) * 32, :] = new[i + 1, FACES[i], :]


def gather_kernel(theta, ot, cell, there, rows):
    for b in range(PB):
        at = slice(b * BLK, (b + 1) * BLK)
        hi, lo = split2(theta[at, :].T)
        rows[0:128, at] = hi
        rows[128:256, at] = lo
    for j in range(4):
        g = dot(rows[...], ot[:, j * 256 : (j + 1) * 256])
        store_pair(there, j, pick(lane_mask(cell, j), g[0:128, :] + g[128:256, :]))


def prepare_kernel(rate, blocks, rc, halves):
    for b in range(PB):
        rc[b * BLK : (b + 1) * BLK, :] = jnp.broadcast_to(rate[b : b + 1, :], (BLK, NR)).T
        for k in range(4):
            hi, lo = split2(blocks[b, k].T)
            halves[b, k * 256 : k * 256 + 128, :] = hi
            halves[b, k * 256 + 128 : k * 256 + 256, :] = lo


def temp_now(b, at, blocks, prof, base, flow):
    added = jnp.concatenate([jnp.zeros((NR - SHELL, BLK), F32), flow[:, at]], axis=0).T
    alive = flag(b < blocks)
    return alive * (base[at, :] + added) + (1.0 - alive) * prof[0, at, :]


def mix_kernel(first, last, *refs):
    if first:
        live, prof, radial, rc, *refs = refs
    else:
        live, prof, radial, rc, base_in, flow, conc_in, *refs = refs
    if last:
        pops, base, out, lattice, conc_new, sems = refs
    else:
        base, ttb, conc_new = refs
    blocks = live[0] // BLK
    wide = []
    for c in range(2):
        hi, lo = split2(radial[c])
        top = jnp.concatenate([hi, lo], axis=1)
        wide.append(jnp.concatenate([top, jnp.concatenate([hi, jnp.zeros_like(hi)], axis=1)], axis=0))
    copies = []
    if last:
        parts = [(0, slice(0, CX), 0, 32), (1, slice(1, CX), 0, 32), (2, slice(0, CX - 1), 0, 32)]
        parts += [(3, slice(0, CX), 8, 32), (4, slice(0, CX), 0, 24), (5, slice(0, CX), 0, 32), (6, slice(0, CX), 0, 32)]
        for n, (i, x, y0, y1) in enumerate(parts):
            at = pl.ds(x.start, x.stop - x.start), pl.ds(y0, y1 - y0)
            copies.append(pltpu.make_async_copy(pops.at[i, *at, :], lattice.at[i, *at, :], sems.at[4 + n]))
            copies[-1].start()
    for b in range(PB):
        at = slice(b * BLK, (b + 1) * BLK)
        conc = prof[1, at, :] if first else conc_in[at, :]
        temp = prof[0, at, :] if first else temp_now(b, at, blocks, prof, base_in, flow)
        alive = flag(b < blocks)
        rate = rc[at, :] * conc * jnp.exp(0.5 * jnp.tanh(temp - 1.0))
        value = halves_of(dot(jnp.concatenate(split2(temp), axis=1), wide[0])) + rate
        base[at, :] = value
        if not last:
            ttb[:, at] = value.T[NR - SHELL :, :]
        value = halves_of(dot(jnp.concatenate(split2(conc), axis=1), wide[1])) - rate
        conc_new[at, :] = alive * value + (1.0 - alive) * conc
        if last and b % 2 == 1:
            two = pl.ds((b - 1) * BLK, 2 * BLK)
            copies.append(pltpu.make_async_copy(conc_new.at[two, :], out.at[1, two, :], sems.at[b // 2]))
            copies[-1].start()
    for copy in copies:
        copy.wait()


def extend(blocks, tt, rxu, rxd, ryu, ryd, extended):
    for b in range(PB):
        alive = flag(b < blocks)
        hi, lo = split2(tt[:, b * BLK : (b + 1) * BLK] * alive)
        extended[b, 0:16, :] = hi
        extended[b, 16:32, :] = lo
        extended[b, 32:48, :] = jnp.full((16, 128), alive, F32).astype(BF16)
    places = ((ryd, 48), (rxd, 16), (ryu, 48), (ryd, 0), (ryu, 0), (ryd, 64), (rxu, 16), (ryu, 64))
    for n in range(8):
        ref, start = places[n]
        there = neighbour(n)
        hi, lo = split2(ref[start : start + 16, :] * there)
        extended[8 + n, 0:16, :] = hi
        extended[8 + n, 16:32, :] = lo
        extended[8 + n, 32:48, :] = jnp.full((16, 128), there, F32).astype(BF16)


def contact_part(cols, ex, tt, halves, extended, store):
    row = lax.broadcasted_iota(jnp.int32, (16, 128), 0)
    for b in range(PB):
        at = slice(b * BLK, (b + 1) * BLK)
        picked = [extended[cols[k // 2, b]] for k in range(8)]
        total = dot(jnp.concatenate(picked, axis=1), halves[b])
        flow = total[0:16, :] + total[16:32, :] - total[32:33, :] * tt[:, at]
        store(b, at, jnp.where(row == 15, flow + ex[b : b + 1, :], flow))


def middle_kernel(
    live, cols_in, ex_in, tt_in, ttb, halves, rxu, rxd, ryu, ryd, theta_in, there_in, edge, cell, coef, otf, lists,
    flow, tt, theta, faces, ex, vt, xu, xd, yu, yd, extended, cols, sem,
):
    fetch = pltpu.make_async_copy(cols_in, cols, sem)
    fetch.start()
    blocks = live[0] // BLK
    extend(blocks, tt_in, rxu, rxd, ryu, ryd, extended)
    theta[...] = theta_in[...]
    came = ((rxd, 48, 1), (rxu, 48, 6), (ryd, 16, 3), (ryu, 16, 4))
    for f in range(4):
        ref, start, n = came[f]
        face = ref[start : start + 32, :] * neighbour(n)
        faces[f * 32 : (f + 1) * 32, :] = face
        theta[FACES[f], :] = theta[FACES[f], :] + face
    rows = jnp.concatenate(split2(faces[...].T), axis=1)
    there = []
    for j in range(4):
        more = pick(lane_mask(cell, j), dot(rows, otf[:, j * 256 : (j + 1) * 256]))
        there.append(pair(there_in, j) + more)
    fetch.wait()

    def store(b, at, value):
        flow[:, at] = value
        alive = flag(b < blocks)
        tt[:, at] = alive * (ttb[:, at] + value) + (1.0 - alive) * tt_in[:, at]

    contact_part(cols, ex_in, tt_in, halves, extended, store)
    send_ghosts(tt, lists, xu, xd, yu, yd)
    send_faces(there, theta, edge, tt, cell, coef, blocks, otf, ex, vt, xu, xd, yu, yd)


def last_kernel(
    live, cols_in, prof, base, ex, tt, halves, rxu, rxd, ryu, ryd, new, prof_in, pops_in,
    profiles, pops, extended, flow, temp, face1, face2, patch3, patch4, cols, sems,
):
    fetch = pltpu.make_async_copy(cols_in, cols, sems.at[8])
    fetch.start()
    blocks = live[0] // BLK
    face1[...] = rxu[48:80, :] * neighbour(6)
    face2[...] = rxd[48:80, :] * neighbour(1)
    y = lax.broadcasted_iota(jnp.int32, (8, 128), 0)
    for x in range(CX):
        patch3[x] = jnp.where(y == 0, ryu[16 + x : 17 + x, :] * neighbour(4), new[3, x, 0:8, :])
        patch4[x] = jnp.where(y == 7, ryd[16 + x : 17 + x, :] * neighbour(3), new[4, x, 24:32, :])
    copies = [
        pltpu.make_async_copy(face1, pops.at[1, 0], sems.at[0]),
        pltpu.make_async_copy(face2, pops.at[2, CX - 1], sems.at[1]),
        pltpu.make_async_copy(patch3, pops.at[3, :, 0:8, :], sems.at[2]),
        pltpu.make_async_copy(patch4, pops.at[4, :, 24:32, :], sems.at[3]),
    ]
    for c in copies:
        c.start()

    def store(b, at, value):
        flow[:, at] = value
        temp[at, :] = temp_now(b, at, blocks, prof, base, flow)
        if b % 2 == 1:
            two = pl.ds((b - 1) * BLK, 2 * BLK)
            copies.append(pltpu.make_async_copy(temp.at[two, :], profiles.at[0, two, :], sems.at[4 + b // 2]))
            copies[-1].start()

    extend(blocks, tt, rxu, rxd, ryu, ryd, extended)
    fetch.wait()
    contact_part(cols, ex, tt, halves, extended, store)
    for c in copies:
        c.wait()


def call(kernel, name, ins, in_specs, outs, out_specs=None, scratch=(), us=2, aliases=None, mib=8):
    shapes = [jax.ShapeDtypeStruct(s, d) for s, d in outs]
    return pl.pallas_call(
        kernel,
        name=name,
        out_shape=shapes,
        in_specs=in_specs,
        out_specs=[VM] * len(outs) if out_specs is None else out_specs,
        scratch_shapes=list(scratch),
        compiler_params=pltpu.CompilerParams(vmem_limit_bytes=mib * 1024 * 1024),
        input_output_aliases=aliases or {},
        cost_estimate=pl.CostEstimate(flops=us * 10**8, bytes_accessed=us * 3 * 10**6, transcendentals=0),
    )(*ins)


def exchange(axis, to_up, to_down):
    n = lax.axis_size(axis)
    up = [(i, (i + 1) % n) for i in range(n)]
    down = [(j, i) for i, j in up]
    return lax.ppermute(to_up, axis, up), lax.ppermute(to_down, axis, down)


def on_device(
    profiles, radial, rate_const, transfer_coef, live_count, send_lists, cell_index, contact_cols, contact_blocks, populations
):
    blocks = contact_blocks.reshape(PB, 4, BLK, BLK)
    rate = rate_const.reshape(PB, BLK)
    cols = contact_cols.T
    plane, lanes, shells, square = ((SLOTS, 128), F32), ((PB, BLK), F32), ((SHELL, SLOTS), F32), ((128, 128), F32)
    lattice = ((7, CELLS, 128), F32)
    wide = ((256, 1024), BF16)
    sends = [((80, 128), F32)] * 2 + [((48, 128), F32)] * 2
    cols_s = pltpu.SMEM((4, PB), jnp.int32)
    ext_s = pltpu.VMEM((16, 48, 128), BF16)

    stay = [
        pltpu.with_memory_space_constraint(a, pltpu.HBM)
        for a in (
            cell_index.reshape(PB, BLK),
            transfer_coef.reshape(PB, BLK),
            send_lists,
            profiles,
            populations.reshape(7, CELLS, 128),
        )
    ]
    cell, coef, lists, prof, pops, ot, otf, tt, theta, ex, vt, xu, xd, yu, yd = call(
        first_kernel, "first", (live_count, *stay),
        [SM] + [HBM] * 5,
        [((PB, BLK), jnp.int32), lanes, ((PB, BLK), jnp.int32), ((2, SLOTS, NR), F32), lattice, ((CELLS, SLOTS), BF16), wide,
         shells, plane, lanes, wide] + sends,
        scratch=[pltpu.VMEM((256, 1024), F32), pltpu.VMEM(*wide), pltpu.VMEM((128, 128), F32),
                 pltpu.SemaphoreType.DMA((5 + CHUNKS,))],
        us=6,
    )
    faces = base = flow = conc = there = edge = None
    for step in range(STEPS):
        final = step == STEPS - 1
        rxu, rxd = exchange("gx", xu, xd)
        inputs = (() if step == 0 else (faces,)) + (pops, theta, vt, ot)
        outs = [lattice] if final else [lattice, plane, square]
        streamed = call(
            functools.partial(stream_kernel, final, step > 0), "stream",
            inputs, [VM] * len(inputs), outs, scratch=[pltpu.VMEM(*plane)], us=3,
        )
        rxu, rxd, streamed = lax.optimization_barrier((rxu, rxd, streamed))
        ryu, ryd = exchange(
            "gy",
            jnp.concatenate([yu, rxd[32:48], rxu[32:48]], axis=0),
            jnp.concatenate([yd, rxd[0:16], rxu[0:16]], axis=0),
        )
        if step == 0:
            rc, halves = call(
                prepare_kernel, "prepare", (rate, blocks), [VM, VM], [plane, ((PB, 1024, BLK), BF16)], us=1
            )
        inputs = (live_count, prof, radial, rc) + (() if step == 0 else (base, flow, conc))
        if final:
            streamed = [streamed[0].reshape(7, CX, 32, 128)]
            inputs = (*inputs, *streamed)
            outs, specs = [plane, ((2, SLOTS, NR), F32), ((7, CX, 32, 128), F32)], [VM, HBM, HBM]
            scratch = [pltpu.VMEM(*plane), pltpu.SemaphoreType.DMA((11,))]
        else:
            outs, specs, scratch = [plane, shells, plane], None, []
        mixed = call(
            functools.partial(mix_kernel, step == 0, final), "mix",
            inputs, [SM] + [VM] * (len(inputs) - 1), outs, out_specs=specs, scratch=scratch, us=1,
        )
        received = (rxu, rxd, ryu, ryd)
        if final:
            return call(
                last_kernel, "last",
                (live_count, cols, prof, mixed[0], ex, tt, halves, *received, *streamed,
                 mixed[1], mixed[2]),
                [SM] + [VM] * 11 + [HBM] * 2,
                [((2, SLOTS, NR), F32), ((7, CX, 32, 128), F32)],
                out_specs=[HBM, HBM],
                scratch=[ext_s, pltpu.VMEM(*shells), pltpu.VMEM(*plane)] + [pltpu.VMEM((32, 128), F32)] * 2
                + [pltpu.VMEM((CX, 8, 128), F32)] * 2 + [cols_s, pltpu.SemaphoreType.DMA((9,))],
                aliases={12: 0, 13: 1},
            )
        base, ttb, conc = mixed
        pops, theta, edge = streamed
        (there,) = call(
            gather_kernel, "gather", (theta, ot, cell), [VM] * 3, [lanes], scratch=[pltpu.VMEM(*wide)], us=1
        )
        flow, tt, theta, faces, ex, vt, xu, xd, yu, yd = call(
            middle_kernel, "middle",
            (live_count, cols, ex, tt, ttb, halves, *received, theta, there, edge, cell, coef, otf, lists),
            [SM] + [VM] * 16,
            [shells, shells, plane, square, lanes, wide] + sends,
            scratch=[ext_s, cols_s, pltpu.SemaphoreType.DMA],
        )


def solution(mesh):
    return jax.shard_map(
        on_device,
        mesh=mesh,
        in_specs=(
            P(None, ("gx", "gy"), None),
            P(),
            P(("gx", "gy")),
            P(("gx", "gy")),
            P(("gx", "gy")),
            P(("gx", "gy"), None),
            P(("gx", "gy")),
            P(("gx", "gy"), None),
            P(("gx", "gy"), None, None, None),
            P(None, "gx", "gy", None),
        ),
        out_specs=(P(None, ("gx", "gy"), None), P(None, "gx", "gy", None)),
        check_vma=False,
    )
```

```python
import functools

import jax
import jax.numpy as jnp
from jax import lax
from jax.experimental import pallas as pl
from jax.experimental.pallas import tpu as pltpu
from jax.sharding import PartitionSpec as P

NR = 128
BLK = 128
SHELL = 16
STEPS = 3
PB = 8
SLOTS = PB * BLK
CX = 32
CELLS = 1024
CHUNKS = 4
CHUNK = CELLS // CHUNKS
PARTS = ((0, 512), (512, 1024))
F32 = jnp.float32
BF16 = jnp.bfloat16

OFFSETS = ((-1, -1), (-1, 0), (-1, 1), (0, -1), (0, 1), (1, -1), (1, 0), (1, 1))
NT = (((1,), (1,)), ((), ()))
NN = (((1,), (0,)), ((), ()))
VM = pl.BlockSpec(memory_space=pltpu.VMEM)
SM = pl.BlockSpec(memory_space=pltpu.SMEM)
HBM = pl.BlockSpec(memory_space=pltpu.HBM)

FACES = (slice(992, 1024), slice(0, 32), pl.ds(31, 32, stride=32), pl.ds(0, 32, stride=32))


def dot(a, b, dims=NN):
    return lax.dot_general(a, b, dims, preferred_element_type=F32)


def split2(x):
    hi = x.astype(BF16)
    return hi, (x - hi.astype(F32)).astype(BF16)


def split3(x):
    hi = x.astype(BF16)
    rest = x - hi.astype(F32)
    mid = rest.astype(BF16)
    return hi, mid, (rest - mid.astype(F32)).astype(BF16)


def flag(cond):
    return jnp.where(cond, 1.0, 0.0).astype(F32)


def neighbour(n):
    a, b = OFFSETS[n]
    x, y = lax.axis_index("gx") - a, lax.axis_index("gy") - b
    return flag((x >= 0) & (x < lax.axis_size("gx")) & (y >= 0) & (y < lax.axis_size("gy")))


def halves_of(g):
    return g[:, 0:128] + g[:, 128:256]


def pair(ref, j):
    return jnp.concatenate([ref[2 * j : 2 * j + 1, :], ref[2 * j + 1 : 2 * j + 2, :]], axis=1)


def store_pair(ref, j, row):
    ref[2 * j : 2 * j + 1, :] = row[:, 0:128]
    ref[2 * j + 1 : 2 * j + 2, :] = row[:, 128:256]


def lane_mask(cell, j):
    return lax.broadcasted_iota(jnp.int32, (128, 256), 0) == (pair(cell, j) & 127)


def pick(mask, g):
    return jnp.sum(jnp.where(mask, g, 0.0), axis=0, keepdims=True)


def send_ghosts(tt, lists, xu, xd, yu, yd):
    places = ((xd, 0), (xd, 16), (xd, 32), (yd, 0), (yu, 0), (xu, 0), (xu, 16), (xu, 32))
    for n in range(8):
        listed = jnp.broadcast_to(lists[n : n + 1, :], (8, BLK))
        lane, block = listed & 127, listed >> 7
        ref, start = places[n]
        for h in (0, 8):
            total = None
            for b in range(PB):
                shell = tt[h : h + 8, b * BLK : (b + 1) * BLK]
                g = jnp.take_along_axis(shell, lane, axis=1, mode="promise_in_bounds")
                total = g if b == 0 else jnp.where(block == b, g, total)
            ref[start + h : start + h + 8, :] = total


def send_faces(there, theta, edge, tt, cell, coef, blocks, otf, ex, vt, xu, xd, yu, yd):
    for j in range(4):
        at = slice(j * 256, (j + 1) * 256)
        alive = jnp.concatenate(
            [jnp.full((1, 128), flag(2 * j + h < blocks), F32) for h in range(2)], axis=1
        )
        e = pair(coef, j) * (there[j] - tt[15:16, at]) * alive
        store_pair(ex, j, e)
        hi, lo = split2(jnp.where(lane_mask(cell, j), e, 0.0))
        vt[0:128, at] = hi
        vt[128:256, at] = lo
    source = halves_of(dot(otf[0:128, :], vt[...], NT))
    outs = ((xu, 48), (xd, 48), (yu, 16), (yd, 16))
    for f in range(4):
        ref, start = outs[f]
        rows = slice(f * 32, (f + 1) * 32)
        s = 1.25 * theta[FACES[f], :] - 0.5 * source[rows, :]
        ref[start : start + 32, :] = 0.125 * s - 0.25 * edge[rows, :]


def first_kernel(
    live, cell_in, coef_in, lists_in, prof_in, pops_in,
    cell, coef, lists, prof, pops, ot, otf, tt, theta, ex, vt, xu, xd, yu, yd,
    gathered, rows, edge, sems,
):
    blocks = live[0] // BLK
    copies = [
        pltpu.make_async_copy(cell_in, cell, sems.at[0]),
        pltpu.make_async_copy(lists_in, lists, sems.at[1]),
        pltpu.make_async_copy(prof_in.at[0], prof.at[0], sems.at[2]),
    ]
    for c, (start, stop) in enumerate(PARTS):
        part = pl.ds(start, stop - start)
        copies.append(pltpu.make_async_copy(pops_in.at[:, part, :], pops.at[:, part, :], sems.at[3 + c]))
    copies.append(pltpu.make_async_copy(coef_in, coef, sems.at[3 + len(PARTS)]))
    copies.append(pltpu.make_async_copy(prof_in.at[1], prof.at[1], sems.at[4 + len(PARTS)]))
    for c in copies:
        c.start()
    sub = lax.broadcasted_iota(jnp.int32, (CELLS, BLK), 0)
    f = lax.broadcasted_iota(jnp.int32, (128, BLK), 0)
    f_row = jnp.where(f < 32, f + 992, jnp.where(f < 64, f - 32, jnp.where(f < 96, f * 32 - 2017, f * 32 - 3072)))
    copies[0].wait()
    for b in range(PB):
        at = slice(b * BLK, (b + 1) * BLK)
        row = cell[b : b + 1, :] >> 7
        ot[:, at] = jnp.where(sub == row, 1.0, 0.0).astype(BF16)
        face = jnp.where(f_row == row, 1.0, 0.0).astype(BF16)
        otf[0:128, at] = face
        otf[128:256, at] = face
    copies[1].wait()
    copies[2].wait()
    for b in range(PB):
        at = slice(b * BLK, (b + 1) * BLK)
        tt[:, at] = prof[0, at, :].T[NR - SHELL :, :]
    send_ghosts(tt, lists, xu, xd, yu, yd)
    for c, (start, stop) in enumerate(PARTS):
        copies[3 + c].wait()
        for h in range(start, stop, 128):
            at = slice(h, h + 128)
            total = pops[0, at, :]
            for i in range(1, 7):
                total = total + pops[i, at, :]
            theta[at, :] = total
            hi, lo = split2(total.T)
            rows[0:128, at] = hi
            rows[128:256, at] = lo
        if stop < CELLS:
            for j in range(4):
                at = slice(j * 256, (j + 1) * 256)
                gathered[:, at] = dot(rows[:, 0:stop], ot[0:stop, at])
    for i in range(4):
        edge[i * 32 : (i + 1) * 32, :] = pops[i + 1, FACES[i], :]
    copies[3 + len(PARTS)].wait()
    there = []
    for j in range(4):
        at = slice(j * 256, (j + 1) * 256)
        g = gathered[:, at] + dot(rows[:, PARTS[-1][0] :], ot[PARTS[-1][0] :, at])
        there.append(pick(lane_mask(cell, j), g[0:128, :] + g[128:256, :]))
    send_faces(there, theta, edge, tt, cell, coef, blocks, otf, ex, vt, xu, xd, yu, yd)
    copies[4 + len(PARTS)].wait()


def stream_kernel(last, has_faces, *refs):
    if has_faces:
        faces, refs = refs[0], refs[1:]
    if last:
        pops, theta, vt, ot, new, source = refs
    else:
        pops, theta, vt, ot, new, theta_new, edge, source = refs
    for j in range(4):
        at = slice(j * 256, (j + 1) * 256)
        source[at, :] = 1.25 * theta[at, :] - 0.5 * halves_of(dot(ot[at, :], vt[...], NT))
    y = lax.broadcasted_iota(jnp.int32, (32, 128), 0)
    z = lax.broadcasted_iota(jnp.int32, (32, 128), 1)

    def row(x, _):
        at = pl.ds(pl.multiple_of(x * 32, 32), 32)
        before = pl.ds(pl.multiple_of(jnp.maximum(x - 1, 0) * 32, 32), 32)
        after = pl.ds(pl.multiple_of(jnp.minimum(x + 1, CX - 1) * 32, 32), 32)
        s = 0.125 * source[at, :]
        n0 = 2.0 * s - 0.25 * pops[0, at, :]
        new[0, at, :] = n0
        n1 = flag(x > 0) * (0.125 * source[before, :] - 0.25 * pops[1, before, :])
        new[1, at, :] = n1
        n2 = flag(x < CX - 1) * (0.125 * source[after, :] - 0.25 * pops[2, after, :])
        new[2, at, :] = n2
        n3 = jnp.where(y == 0, 0.0, pltpu.roll(s - 0.25 * pops[3, at, :], 1, 0))
        new[3, at, :] = n3
        n4 = jnp.where(y == 31, 0.0, pltpu.roll(s - 0.25 * pops[4, at, :], 31, 0))
        new[4, at, :] = n4
        n5 = jnp.where(z == 0, 0.0, pltpu.roll(s - 0.25 * pops[5, at, :], 1, 1))
        new[5, at, :] = n5
        n6 = jnp.where(z == 127, 0.0, pltpu.roll(s - 0.25 * pops[6, at, :], 127, 1))
        new[6, at, :] = n6
        if not last:
            theta_new[at, :] = ((n0 + n1) + (n2 + n3)) + ((n4 + n5) + n6)
        return 0

    def carry_faces(c):
        parts = (
            (0, 1, slice(32, 64), faces[32:64, :]),
            (CHUNKS - 1, 2, slice(960, 992), faces[0:32, :]),
            (c, 3, pl.ds(c * CHUNK + 1, 8, stride=32), faces[96 + c * 8 : 104 + c * 8, :]),
            (c, 4, pl.ds(c * CHUNK + 30, 8, stride=32), faces[64 + c * 8 : 72 + c * 8, :]),
        )
        for chunk, i, at, face in parts:
            if chunk == c:
                new[i, at, :] = new[i, at, :] - 0.25 * face
                if not last:
                    theta_new[at, :] = theta_new[at, :] - 0.25 * face

    for c in range(CHUNKS):
        lax.fori_loop(c * 8, (c + 1) * 8, row, 0, unroll=2)
        if has_faces:
            carry_faces(c)
    if last:
        return
    for i in range(4):
        edge[i * 32 : (i + 1) * 32, :] = new[i + 1, FACES[i], :]


def gather_kernel(theta, ot, cell, there, rows):
    for b in range(PB):
        at = slice(b * BLK, (b + 1) * BLK)
        hi, lo = split2(theta[at, :].T)
        rows[0:128, at] = hi
        rows[128:256, at] = lo
    for j in range(4):
        g = dot(rows[...], ot[:, j * 256 : (j + 1) * 256])
        store_pair(there, j, pick(lane_mask(cell, j), g[0:128, :] + g[128:256, :]))


def prepare_kernel(rate, blocks, rc, halves):
    for b in range(PB):
        rc[b * BLK : (b + 1) * BLK, :] = jnp.broadcast_to(rate[b : b + 1, :], (BLK, NR)).T
        for k in range(4):
            hi, lo = split2(blocks[b, k].T)
            halves[b, k * 256 : k * 256 + 128, :] = hi
            halves[b, k * 256 + 128 : k * 256 + 256, :] = lo


def temp_now(b, at, blocks, prof, base, flow):
    added = jnp.concatenate([jnp.zeros((NR - SHELL, BLK), F32), flow[:, at]], axis=0).T
    alive = flag(b < blocks)
    return alive * (base[at, :] + added) + (1.0 - alive) * prof[0, at, :]


def mix_kernel(first, last, *refs):
    if first:
        live, prof, radial, rc, *refs = refs
    else:
        live, prof, radial, rc, base_in, flow, conc_in, *refs = refs
    if last:
        pops, base, out, lattice, conc_new, sems = refs
    else:
        base, ttb, conc_new = refs
    blocks = live[0] // BLK
    wide = []
    for c in range(2):
        hi, lo = split2(radial[c])
        top = jnp.concatenate([hi, lo], axis=1)
        wide.append(jnp.concatenate([top, jnp.concatenate([hi, jnp.zeros_like(hi)], axis=1)], axis=0))
    copies = []
    if last:
        parts = [(0, slice(0, CX), 0, 32), (1, slice(1, CX), 0, 32), (2, slice(0, CX - 1), 0, 32)]
        parts += [(3, slice(0, CX), 8, 32), (4, slice(0, CX), 0, 24), (5, slice(0, CX), 0, 32), (6, slice(0, CX), 0, 32)]
        for n, (i, x, y0, y1) in enumerate(parts):
            at = pl.ds(x.start, x.stop - x.start), pl.ds(y0, y1 - y0)
            copies.append(pltpu.make_async_copy(pops.at[i, *at, :], lattice.at[i, *at, :], sems.at[4 + n]))
            copies[-1].start()
    for b in range(PB):
        at = slice(b * BLK, (b + 1) * BLK)
        conc = prof[1, at, :] if first else conc_in[at, :]
        temp = prof[0, at, :] if first else temp_now(b, at, blocks, prof, base_in, flow)
        alive = flag(b < blocks)
        rate = rc[at, :] * conc * jnp.exp(0.5 * jnp.tanh(temp - 1.0))
        value = halves_of(dot(jnp.concatenate(split2(temp), axis=1), wide[0])) + rate
        base[at, :] = value
        if not last:
            ttb[:, at] = value.T[NR - SHELL :, :]
        value = halves_of(dot(jnp.concatenate(split2(conc), axis=1), wide[1])) - rate
        conc_new[at, :] = alive * value + (1.0 - alive) * conc
        if last and b % 2 == 1:
            two = pl.ds((b - 1) * BLK, 2 * BLK)
            copies.append(pltpu.make_async_copy(conc_new.at[two, :], out.at[1, two, :], sems.at[b // 2]))
            copies[-1].start()
    for copy in copies:
        copy.wait()


def extend(blocks, tt, rxu, rxd, ryu, ryd, extended):
    for b in range(PB):
        alive = flag(b < blocks)
        hi, lo = split2(tt[:, b * BLK : (b + 1) * BLK] * alive)
        extended[b, 0:16, :] = hi
        extended[b, 16:32, :] = lo
        extended[b, 32:48, :] = jnp.full((16, 128), alive, F32).astype(BF16)
    places = ((ryd, 48), (rxd, 16), (ryu, 48), (ryd, 0), (ryu, 0), (ryd, 64), (rxu, 16), (ryu, 64))
    for n in range(8):
        ref, start = places[n]
        there = neighbour(n)
        hi, lo = split2(ref[start : start + 16, :] * there)
        extended[8 + n, 0:16, :] = hi
        extended[8 + n, 16:32, :] = lo
        extended[8 + n, 32:48, :] = jnp.full((16, 128), there, F32).astype(BF16)


def contact_part(cols, ex, tt, halves, extended, store):
    row = lax.broadcasted_iota(jnp.int32, (16, 128), 0)
    for b in range(PB):
        at = slice(b * BLK, (b + 1) * BLK)
        picked = [extended[cols[k // 2, b]] for k in range(8)]
        total = dot(jnp.concatenate(picked, axis=1), halves[b])
        flow = total[0:16, :] + total[16:32, :] - total[32:33, :] * tt[:, at]
        store(b, at, jnp.where(row == 15, flow + ex[b : b + 1, :], flow))


def middle_kernel(
    live, cols_in, ex_in, tt_in, ttb, halves, rxu, rxd, ryu, ryd, theta_in, there_in, edge, cell, coef, otf, lists,
    flow, tt, theta, faces, ex, vt, xu, xd, yu, yd, extended, cols, sem,
):
    fetch = pltpu.make_async_copy(cols_in, cols, sem)
    fetch.start()
    blocks = live[0] // BLK
    extend(blocks, tt_in, rxu, rxd, ryu, ryd, extended)
    theta[...] = theta_in[...]
    came = ((rxd, 48, 1), (rxu, 48, 6), (ryd, 16, 3), (ryu, 16, 4))
    for f in range(4):
        ref, start, n = came[f]
        face = ref[start : start + 32, :] * neighbour(n)
        faces[f * 32 : (f + 1) * 32, :] = face
        theta[FACES[f], :] = theta[FACES[f], :] + face
    rows = jnp.concatenate(split2(faces[...].T), axis=1)
    there = []
    for j in range(4):
        more = pick(lane_mask(cell, j), dot(rows, otf[:, j * 256 : (j + 1) * 256]))
        there.append(pair(there_in, j) + more)
    fetch.wait()

    def store(b, at, value):
        flow[:, at] = value
        alive = flag(b < blocks)
        tt[:, at] = alive * (ttb[:, at] + value) + (1.0 - alive) * tt_in[:, at]

    contact_part(cols, ex_in, tt_in, halves, extended, store)
    send_ghosts(tt, lists, xu, xd, yu, yd)
    send_faces(there, theta, edge, tt, cell, coef, blocks, otf, ex, vt, xu, xd, yu, yd)


def last_kernel(
    live, cols_in, prof, base, ex, tt, halves, rxu, rxd, ryu, ryd, new, prof_in, pops_in,
    profiles, pops, extended, flow, temp, face1, face2, patch3, patch4, cols, sems,
):
    fetch = pltpu.make_async_copy(cols_in, cols, sems.at[8])
    fetch.start()
    blocks = live[0] // BLK
    face1[...] = rxu[48:80, :] * neighbour(6)
    face2[...] = rxd[48:80, :] * neighbour(1)
    y = lax.broadcasted_iota(jnp.int32, (8, 128), 0)
    for x in range(CX):
        patch3[x] = jnp.where(y == 0, ryu[16 + x : 17 + x, :] * neighbour(4), new[3, x, 0:8, :])
        patch4[x] = jnp.where(y == 7, ryd[16 + x : 17 + x, :] * neighbour(3), new[4, x, 24:32, :])
    copies = [
        pltpu.make_async_copy(face1, pops.at[1, 0], sems.at[0]),
        pltpu.make_async_copy(face2, pops.at[2, CX - 1], sems.at[1]),
        pltpu.make_async_copy(patch3, pops.at[3, :, 0:8, :], sems.at[2]),
        pltpu.make_async_copy(patch4, pops.at[4, :, 24:32, :], sems.at[3]),
    ]
    for c in copies:
        c.start()

    def store(b, at, value):
        flow[:, at] = value
        temp[at, :] = temp_now(b, at, blocks, prof, base, flow)
        if b % 2 == 1:
            two = pl.ds((b - 1) * BLK, 2 * BLK)
            copies.append(pltpu.make_async_copy(temp.at[two, :], profiles.at[0, two, :], sems.at[4 + b // 2]))
            copies[-1].start()

    extend(blocks, tt, rxu, rxd, ryu, ryd, extended)
    fetch.wait()
    contact_part(cols, ex, tt, halves, extended, store)
    for c in copies:
        c.wait()


def call(kernel, name, ins, in_specs, outs, out_specs=None, scratch=(), us=2, aliases=None, mib=8):
    shapes = [jax.ShapeDtypeStruct(s, d) for s, d in outs]
    return pl.pallas_call(
        kernel,
        name=name,
        out_shape=shapes,
        in_specs=in_specs,
        out_specs=[VM] * len(outs) if out_specs is None else out_specs,
        scratch_shapes=list(scratch),
        compiler_params=pltpu.CompilerParams(vmem_limit_bytes=mib * 1024 * 1024),
        input_output_aliases=aliases or {},
        cost_estimate=pl.CostEstimate(flops=us * 10**8, bytes_accessed=us * 3 * 10**6, transcendentals=0),
    )(*ins)


def exchange(axis, to_up, to_down):
    n = lax.axis_size(axis)
    up = [(i, (i + 1) % n) for i in range(n)]
    down = [(j, i) for i, j in up]
    return lax.ppermute(to_up, axis, up), lax.ppermute(to_down, axis, down)


def on_device(
    profiles, radial, rate_const, transfer_coef, live_count, send_lists, cell_index, contact_cols, contact_blocks, populations
):
    blocks = contact_blocks.reshape(PB, 4, BLK, BLK)
    rate = rate_const.reshape(PB, BLK)
    cols = contact_cols.T
    plane, lanes, shells, square = ((SLOTS, 128), F32), ((PB, BLK), F32), ((SHELL, SLOTS), F32), ((128, 128), F32)
    lattice = ((7, CELLS, 128), F32)
    wide = ((256, 1024), BF16)
    sends = [((80, 128), F32)] * 2 + [((48, 128), F32)] * 2
    cols_s = pltpu.SMEM((4, PB), jnp.int32)
    ext_s = pltpu.VMEM((16, 48, 128), BF16)

    stay = [
        pltpu.with_memory_space_constraint(a, pltpu.HBM)
        for a in (
            cell_index.reshape(PB, BLK),
            transfer_coef.reshape(PB, BLK),
            send_lists,
            profiles,
            populations.reshape(7, CELLS, 128),
        )
    ]
    cell, coef, lists, prof, pops, ot, otf, tt, theta, ex, vt, xu, xd, yu, yd = call(
        first_kernel, "first", (live_count, *stay),
        [SM] + [HBM] * 5,
        [((PB, BLK), jnp.int32), lanes, ((PB, BLK), jnp.int32), ((2, SLOTS, NR), F32), lattice, ((CELLS, SLOTS), BF16), wide,
         shells, plane, lanes, wide] + sends,
        scratch=[pltpu.VMEM((256, 1024), F32), pltpu.VMEM(*wide), pltpu.VMEM((128, 128), F32),
                 pltpu.SemaphoreType.DMA((5 + len(PARTS),))],
        us=6,
    )
    faces = base = flow = conc = there = edge = None
    for step in range(STEPS):
        final = step == STEPS - 1
        rxu, rxd = exchange("gx", xu, xd)
        inputs = (() if step == 0 else (faces,)) + (pops, theta, vt, ot)
        outs = [lattice] if final else [lattice, plane, square]
        streamed = call(
            functools.partial(stream_kernel, final, step > 0), "stream",
            inputs, [VM] * len(inputs), outs, scratch=[pltpu.VMEM(*plane)], us=3,
        )
        rxu, rxd, streamed = lax.optimization_barrier((rxu, rxd, streamed))
        ryu, ryd = exchange(
            "gy",
            jnp.concatenate([yu, rxd[32:48], rxu[32:48]], axis=0),
            jnp.concatenate([yd, rxd[0:16], rxu[0:16]], axis=0),
        )
        if step == 0:
            rc, halves = call(
                prepare_kernel, "prepare", (rate, blocks), [VM, VM], [plane, ((PB, 1024, BLK), BF16)], us=1
            )
        inputs = (live_count, prof, radial, rc) + (() if step == 0 else (base, flow, conc))
        if final:
            streamed = [streamed[0].reshape(7, CX, 32, 128)]
            inputs = (*inputs, *streamed)
            outs, specs = [plane, ((2, SLOTS, NR), F32), ((7, CX, 32, 128), F32)], [VM, HBM, HBM]
            scratch = [pltpu.VMEM(*plane), pltpu.SemaphoreType.DMA((11,))]
        else:
            outs, specs, scratch = [plane, shells, plane], None, []
        mixed = call(
            functools.partial(mix_kernel, step == 0, final), "mix",
            inputs, [SM] + [VM] * (len(inputs) - 1), outs, out_specs=specs, scratch=scratch, us=1,
        )
        received = (rxu, rxd, ryu, ryd)
        if final:
            return call(
                last_kernel, "last",
                (live_count, cols, prof, mixed[0], ex, tt, halves, *received, *streamed,
                 mixed[1], mixed[2]),
                [SM] + [VM] * 11 + [HBM] * 2,
                [((2, SLOTS, NR), F32), ((7, CX, 32, 128), F32)],
                out_specs=[HBM, HBM],
                scratch=[ext_s, pltpu.VMEM(*shells), pltpu.VMEM(*plane)] + [pltpu.VMEM((32, 128), F32)] * 2
                + [pltpu.VMEM((CX, 8, 128), F32)] * 2 + [cols_s, pltpu.SemaphoreType.DMA((9,))],
                aliases={12: 0, 13: 1},
            )
        base, ttb, conc = mixed
        pops, theta, edge = streamed
        (there,) = call(
            gather_kernel, "gather", (theta, ot, cell), [VM] * 3, [lanes], scratch=[pltpu.VMEM(*wide)], us=1
        )
        flow, tt, theta, faces, ex, vt, xu, xd, yu, yd = call(
            middle_kernel, "middle",
            (live_count, cols, ex, tt, ttb, halves, *received, theta, there, edge, cell, coef, otf, lists),
            [SM] + [VM] * 16,
            [shells, shells, plane, square, lanes, wide] + sends,
            scratch=[ext_s, cols_s, pltpu.SemaphoreType.DMA],
        )


def solution(mesh):
    return jax.shard_map(
        on_device,
        mesh=mesh,
        in_specs=(
            P(None, ("gx", "gy"), None),
            P(),
            P(("gx", "gy")),
            P(("gx", "gy")),
            P(("gx", "gy")),
            P(("gx", "gy"), None),
            P(("gx", "gy")),
            P(("gx", "gy"), None),
            P(("gx", "gy"), None, None, None),
            P(None, "gx", "gy", None),
        ),
        out_specs=(P(None, ("gx", "gy"), None), P(None, "gx", "gy", None)),
        check_vma=False,
    )
```
